1024 devices in a mesh: ctx: 128 (over z, x, core), head: 8 (over y).
Axes of the slice: x: 8, y: 8, z: 8, core: 2. Of those that a mesh axis runs over, the one named last changes fastest.
Arguments:
- queries: bfloat16 [32768, 16, 128], P('ctx', 'head'), may hold values from -6 to 6
- spikes: int32 [32768, 16, 128], P('ctx', 'head'), may hold values from 0 to 3
- values: bfloat16 [32768, 16, 128], P('ctx', 'head'), may hold values from -6 to 6
- threshold: float32 [128], replicated, may hold values from 0.05 to 0.5
- norm_gain: float32 [128], replicated, may hold values from 0.1 to 1.9
- document_ids: int32 [32768], P('ctx'), may hold values from 0 to 511, never falling along the last dimension, each value on 1 to 8192 neighbouring positions
- cotangent: bfloat16 [32768, 16, 128], P('ctx', 'head'), may hold values from -6 to 6
Outputs:
- attended: bfloat16 [32768, 16, 128], P('ctx', 'head')
- query_grad: bfloat16 [32768, 16, 128], P('ctx', 'head')
- value_grad: bfloat16 [32768, 16, 128], P('ctx', 'head')
- threshold_grad: float32 [128], replicated
- gain_grad: float32 [128], replicated
The draws below stay inside these ranges and needn't reach their ends.
Inputs may be any that keep to these rules, and one draw needn't show every extreme that they name: `document_ids`: ids never fall along the context; each document holds 1 to 8192 consecutive tokens, and one holds exactly 8192.
All inputs are finite; a program needn't handle non-finite values.
Results may differ from the reference program's by a relative error of at most 0.011.
Values sent between devices are 32-bit elements; how exact they have to be, the bound alone decides.
A program may use at most 128 MiB of HBM per device.

```python
import math
import jax
import jax.numpy as jnp
import numpy as np
from jax import lax

DK = 128
TOK_DEV = 256
TOKENS = 32768
HEADS = 16
DOCS = 512
N_CTX = 128


def place_ends(values, rng, low, largest):
    spot = [jax.random.randint(jax.random.fold_in(rng, axis), (), 0, length) for axis, length in enumerate(values.shape)]
    longest = values.shape.index(max(values.shape))
    next_to = spot[:longest] + [(spot[longest] + 1) % values.shape[longest]] + spot[longest + 1:]
    return values.at[tuple(spot)].set(low).at[tuple(next_to)].set(largest)


def levels(stream_key, dims, shards, smallest, top_value):
    level = 1.0
    for dim, shards_of in shards:
        heights = jax.random.uniform(jax.random.fold_in(jax.random.fold_in(stream_key, 6), dim), (shards_of,), jnp.float32, smallest / len(shards), top_value / len(shards))
        level = level * jnp.repeat(jnp.exp(heights), dims[dim] // shards_of).reshape((-1,) + (1,) * (len(dims) - 1 - dim))
    return level


def split_up(number_of, total, most, lean):
    portions = [(1 << 20) // math.isqrt(rank ** lean) + 1 for rank in range(2, number_of + 1)]
    surplus, counts = total - most - (number_of - 1), [1] * (number_of - 1)
    while surplus > 0:
        candidates = [i for i in range(number_of - 1) if counts[i] < most]
        whole, remaining = sum([portions[i] for i in candidates]), surplus
        for i in candidates:
            more = min(most - counts[i], max(1, remaining * portions[i] // whole), surplus)
            counts[i] = counts[i] + more
            surplus = surplus - more
    return np.array([most] + counts)


def uneven_parts(stream_key, number_of, total, reach, skew):
    if number_of == 2:
        one = jax.random.randint(stream_key, (), max(1, total - reach), min(reach, total - 1) + 1)
        return jnp.stack([one, total - one])
    lengths = jnp.asarray(split_up(number_of, total, reach, skew), jnp.int32)
    pairs = (number_of - 1) // 2
    giver, receiver = lengths[1:1 + 2 * pairs:2], lengths[2:2 + 2 * pairs:2]
    room = jnp.minimum(giver - 1, reach - receiver)
    moved = jax.random.randint(jax.random.fold_in(stream_key, 1), (pairs,), 0, 1 << 20) % (room + 1)
    lengths = lengths.at[1:1 + 2 * pairs:2].set(giver - moved).at[2:2 + 2 * pairs:2].set(receiver + moved)
    return lengths[jax.random.permutation(jax.random.fold_in(stream_key, 2), number_of)]


def bell_draw(rng, dims, deviation, reach, pieces=(), held_as=jnp.bfloat16):
    values = jax.random.normal(rng, dims, jnp.float32) * deviation
    if len(pieces) > 0:
        values = levels(rng, dims, pieces, -0.22, 0.18) * values
    return jnp.clip(values, min=-reach, max=reach).astype(held_as)


def setup_inputs(seed: int = 0) -> dict:
    keys = jax.random.split(jax.random.key(seed), 8)
    return {
        "queries": bell_draw(keys[0], (TOKENS, HEADS, DK), 1.0, 6.0, ((0, 128), (1, 8))),
        "spikes": place_ends(jax.random.randint(keys[1], (TOKENS, HEADS, DK), 0, 4), jax.random.fold_in(keys[1], 1), 0, 3).astype(jnp.int32),
        "values": bell_draw(keys[2], (TOKENS, HEADS, DK), 1.0, 6.0, ((0, 128), (1, 8))),
        "threshold": jnp.clip(jnp.exp(jax.random.uniform(keys[3], (DK,), jnp.float32, math.log(0.05), math.log(0.5))), 0.05, 0.5),
        "norm_gain": jnp.clip(1.0 + 0.18 * jax.random.normal(keys[4], (DK,), jnp.float32), 0.1, 1.9),
        "document_ids": jnp.searchsorted(jnp.cumsum(uneven_parts(keys[5], DOCS, TOKENS, TOKENS // 4, 2)), jnp.arange(TOKENS), side="right").astype(jnp.int32),
        "cotangent": bell_draw(keys[6], (TOKENS, HEADS, DK), 1.0, 6.0, ((0, 128), (1, 8))),
    }


def rounded(tensor):
    return lax.optimization_barrier(tensor.astype(jnp.bfloat16)).astype(jnp.float32)

def reference(queries, spikes, values, threshold, norm_gain, document_ids, cotangent):
    keys_bf = (spikes.astype(jnp.float32) * threshold).astype(jnp.bfloat16)
    block_shape = (N_CTX, TOK_DEV, HEADS, DK)
    query_blocks = queries.reshape(block_shape)
    key_blocks = keys_bf.reshape(block_shape)
    value_blocks = values.reshape(block_shape)
    spike_blocks = spikes.reshape(block_shape)
    cot_blocks = cotangent.reshape(block_shape)
    doc_blocks = document_ids.reshape(N_CTX, TOK_DEV)

    def forward_step(carry, items):
        state, marker = carry
        key_c, value_c, doc_c = items
        last_f = (doc_c == doc_c[-1]).astype(jnp.float32)[:, None, None]
        tail = jnp.einsum('thd,the->hde', key_c.astype(jnp.float32) * last_f, value_c.astype(jnp.float32))
        incoming = jnp.where(marker == doc_c[0], state, jnp.float32(0.0)).astype(jnp.bfloat16)
        new_state = tail + jnp.where(marker == doc_c[-1], state, jnp.float32(0.0))
        return ((new_state, doc_c[-1]), incoming)
    start = (jnp.zeros((HEADS, DK, DK), jnp.float32), jnp.int32(-1))
    ignored, carried_all = lax.scan(forward_step, start, (key_blocks, value_blocks, doc_blocks))
    position = jnp.arange(TOK_DEV, dtype=jnp.int32)

    def reverse_step(carry, items):
        state, marker = carry
        query_c, key_c, value_c, spike_c, cot_c, doc_c, carried = items
        qf = query_c.astype(jnp.float32)
        kf = key_c.astype(jnp.float32)
        vf = value_c.astype(jnp.float32)
        allowed = (position[None, :] <= position[:, None]) & (doc_c[:, None] == doc_c[None, :])
        in_first = (doc_c == doc_c[0]).astype(jnp.float32)[:, None, None]
        in_last = (doc_c == doc_c[-1]).astype(jnp.float32)[:, None, None]
        scores = rounded(jnp.where(allowed[None], jnp.einsum('shd,thd->hst', qf, kf), jnp.float32(0.0)))
        carried_f = carried.astype(jnp.float32)
        mixed_raw = qf + jnp.einsum('hst,thd->shd', scores, vf) + in_first * jnp.einsum('shd,hde->she', qf, carried_f)
        ratio = lax.rsqrt(lax.optimization_barrier(jnp.mean(mixed_raw * mixed_raw, axis=-1, keepdims=True)) + 1e-06)
        normed = mixed_raw * ratio
        attended = (normed * norm_gain).astype(jnp.bfloat16)
        cot_f = cot_c.astype(jnp.float32)
        upstream = cot_f * norm_gain
        gnorm = rounded(ratio * upstream - normed * ratio * lax.optimization_barrier(jnp.mean(normed * upstream, axis=-1, keepdims=True)))
        dscores = rounded(jnp.where(allowed[None], jnp.einsum('shd,thd->hst', gnorm, vf), jnp.float32(0.0)))
        tail_ret = jnp.einsum('shd,she->hde', qf * in_first, gnorm)
        returned = rounded(jnp.where(marker == doc_c[-1], state, jnp.float32(0.0)))
        query_grad = gnorm + jnp.einsum('hst,thd->shd', dscores, kf) + in_first * jnp.einsum('she,hde->shd', gnorm, carried_f)
        key_grad = jnp.einsum('hst,shd->thd', dscores, qf) + in_last * jnp.einsum('the,hde->thd', vf, returned)
        value_grad = jnp.einsum('hst,she->the', scores, gnorm) + in_last * jnp.einsum('thd,hde->the', kf, returned)
        thresh_term = lax.optimization_barrier(jnp.sum(spike_c.astype(jnp.float32) * key_grad, axis=(0, 1)))
        gain_term = lax.optimization_barrier(jnp.sum(cot_f * normed, axis=(0, 1)))
        new_state = tail_ret + jnp.where(marker == doc_c[0], state, jnp.float32(0.0))
        outputs = (attended, query_grad.astype(jnp.bfloat16), value_grad.astype(jnp.bfloat16), thresh_term, gain_term)
        return ((new_state, doc_c[0]), outputs)
    items = (query_blocks, key_blocks, value_blocks, spike_blocks, cot_blocks, doc_blocks, carried_all)
    ignored, results = lax.scan(reverse_step, start, items, reverse=True)
    full_shape = (TOKENS, HEADS, DK)
    scale = jnp.float32(1.0) / jnp.sqrt(jnp.float32(TOKENS * HEADS))
    attended = results[0].reshape(full_shape)
    query_grad = results[1].reshape(full_shape)
    value_grad = results[2].reshape(full_shape)
    threshold_grad = lax.optimization_barrier(jnp.sum(results[3], axis=0)) * scale
    gain_grad = lax.optimization_barrier(jnp.sum(results[4], axis=0)) * scale
    return (attended, query_grad, value_grad, threshold_grad, gain_grad)
```

```python
import functools
import math

import jax
import jax.numpy as jnp
from jax import lax
from jax.experimental import pallas as pl
from jax.experimental.pallas import tpu as pltpu
from jax.sharding import PartitionSpec as P

MESH = pl.DeviceIdType.MESH
F32 = jnp.float32
BF16 = jnp.bfloat16

ROW = 16


def mm(a, b, ca, cb):
    return lax.dot_general(a, b, (((ca,), (cb,)), ((), ())), preferred_element_type=F32)


def kernel(
    dims,
    docs_ref,
    thr_ref,
    gain_ref,
    q_hbm,
    spk_hbm,
    v_hbm,
    cot_hbm,
    att_hbm,
    qg_hbm,
    vg_hbm,
    grads_ref,
    q_in,
    spk_in,
    v_in,
    cot_in,
    q_st,
    v_st,
    cot_st,
    docT,
    mask,
    qb,
    kb,
    vb,
    gb,
    scores,
    base,
    vgrad,
    meta_my,
    meta,
    tail_f,
    recv_f,
    send_f,
    zs_f,
    zr_f,
    carr,
    tail_b,
    recv_b,
    send_b,
    zs_b,
    zr_b,
    retn,
    att_st,
    out_st,
    ar_x,
    ar_z,
    ar_y,
    att_out,
    qg_out,
    vg_out,
    in_sem,
    out_sem,
    meta_s,
    meta_r,
    st1_s,
    st1_r,
    st2_s,
    st2_r,
    st3_s,
    st3_r,
    st3_p,
    ar_s,
    ar_r,
):
    n_ctx, n_head, row_n, length, heads, width = dims
    chips = row_n // 2
    n_rows = n_ctx // row_n
    pr = width // chips
    me = lax.axis_index("ctx")
    my_y = lax.axis_index("head")
    my_row = me // row_n
    row0 = my_row * row_n
    pos = me - row0
    my_chip = pos // 2
    my_core = pos - my_chip * 2
    mid = chips // 2

    def peer_chip(t):
        turn = (t + 1) // 2
        d = mid + turn * (1 - 2 * (t - 2 * (t // 2)))
        return lax.rem(my_chip + d, chips)

    def in_row(p):
        return {"ctx": row0 + p}

    def along_z(k):
        return {"ctx": lax.rem(my_row + k, n_rows) * row_n + pos}

    def along_y(k):
        return {"head": lax.rem(my_y + k, n_head)}

    barrier = pltpu.get_barrier_semaphore()

    def greet_row(k, c):
        pl.semaphore_signal(
            barrier, inc=1, device_id=in_row(lax.rem(pos + k, row_n)), device_id_type=MESH
        )
        return c

    def greet_z(k, c):
        pl.semaphore_signal(barrier, inc=1, device_id=along_z(k), device_id_type=MESH)
        return c

    def greet_y(k, c):
        pl.semaphore_signal(barrier, inc=1, device_id=along_y(k), device_id_type=MESH)
        return c

    lax.fori_loop(1, row_n, greet_row, 0)
    lax.fori_loop(1, n_rows, greet_z, 0)
    if n_head > 1:
        lax.fori_loop(1, n_head, greet_y, 0)

    ins = [
        pltpu.make_async_copy(src, dst, in_sem.at[i])
        for i, (src, dst) in enumerate(
            ((spk_hbm, spk_in), (v_hbm, v_in), (q_hbm, q_in), (cot_hbm, cot_in))
        )
    ]
    for cp in ins:
        cp.start()

    doc_row = docs_ref[...].astype(F32)
    docT[...] = jnp.transpose(jnp.broadcast_to(doc_row, (width, length)))
    head_doc = docT[0:1, :]
    tail_doc = docT[length - 1 : length, :]
    sub = lax.broadcasted_iota(jnp.int32, (8, width), 0)
    meta_my[...] = jnp.where(
        sub == 0, jnp.broadcast_to(head_doc, (8, width)), jnp.broadcast_to(tail_doc, (8, width))
    )
    meta[pl.ds(pos, 1)] = meta_my[...].reshape(1, 8, width)
    thr = thr_ref[...]
    gain = gain_ref[...]
    thr_col = jnp.transpose(jnp.broadcast_to(thr, (width, width)))

    n_greet = (row_n - 1) + (n_rows - 1) + (n_head - 1)
    pl.semaphore_wait(barrier, n_greet)

    def send_meta(t, c):
        chip = peer_chip(t)
        for core in range(2):
            pltpu.make_async_remote_copy(
                src_ref=meta_my,
                dst_ref=meta.at[pos],
                send_sem=meta_s,
                recv_sem=meta_r,
                device_id=in_row(chip * 2 + core),
                device_id_type=MESH,
            ).start()
        return c

    lax.fori_loop(0, chips - 1, send_meta, 0)
    pltpu.make_async_remote_copy(
        src_ref=meta_my,
        dst_ref=meta.at[pos],
        send_sem=meta_s,
        recv_sem=meta_r,
        device_id=in_row(my_chip * 2 + 1 - my_core),
        device_id_type=MESH,
    ).start()

    def scatter(h, tail, recv, way):
        def piece(chip):
            return tail.at[pl.ds(h * width + chip * pr, pr)]

        def one(chip):
            pltpu.make_async_remote_copy(
                src_ref=piece(chip),
                dst_ref=recv.at[pos],
                send_sem=st1_s.at[way],
                recv_sem=st1_r.at[way],
                device_id=in_row(chip * 2 + h),
                device_id_type=MESH,
            ).start()

        def body(t, c):
            one(peer_chip(t))
            return c

        lax.fori_loop(0, chips - 1, body, 0)

        @pl.when(my_core != h)
        def _():
            one(my_chip)

        @pl.when(my_core == h)
        def _():
            recv[pl.ds(pos, 1)] = tail[pl.ds(h * width + my_chip * pr, pr), :].reshape(
                1, pr, width
            )

    def scatter_descriptor(recv, way):
        return pltpu.make_async_remote_copy(
            src_ref=recv.at[pl.ds(0, row_n - 1)],
            dst_ref=recv.at[pl.ds(0, row_n - 1)],
            send_sem=st1_s.at[way],
            recv_sem=st1_r.at[way],
            device_id=in_row(lax.rem(pos + 1, row_n)),
            device_id_type=MESH,
        )

    def gather(send, land, way):
        at = my_core * width + my_chip * pr

        def one(p, rsem):
            pltpu.make_async_remote_copy(
                src_ref=send.at[p],
                dst_ref=land.at[pl.ds(at, pr)],
                send_sem=st3_s.at[way],
                recv_sem=rsem,
                device_id=in_row(p),
                device_id_type=MESH,
            ).start()

        def body(t, c):
            chip = peer_chip(t)
            for core in range(2):
                one(chip * 2 + core, st3_r.at[way, my_core])
            return c

        lax.fori_loop(0, chips - 1, body, 0)
        one(my_chip * 2 + 1 - my_core, st3_p.at[way])
        land[pl.ds(at, pr), :] = send[pl.ds(pos, 1)].reshape(pr, width)

    def gather_wait_chips(land, way, h):
        part = land.at[pl.ds(0, (chips - 1) * pr)]
        pltpu.make_async_remote_copy(
            src_ref=part,
            dst_ref=part,
            send_sem=st3_s.at[way],
            recv_sem=st3_r.at[way, h],
            device_id=in_row(lax.rem(pos + 1, row_n)),
            device_id_type=MESH,
        ).wait_recv()

    def gather_wait_partner(land, way):
        part = land.at[pl.ds(0, pr)]
        pltpu.make_async_remote_copy(
            src_ref=part,
            dst_ref=part,
            send_sem=st3_s.at[way],
            recv_sem=st3_p.at[way],
            device_id=in_row(lax.rem(pos + 1, row_n)),
            device_id_type=MESH,
        ).wait_recv()

    def between_rows(k, zs, zr, slot, way):
        return pltpu.make_async_remote_copy(
            src_ref=zs,
            dst_ref=zr.at[slot],
            send_sem=st2_s.at[way, slot],
            recv_sem=st2_r.at[way, slot],
            device_id=along_z(k),
            device_id_type=MESH,
        )

    def with_mark(total, mark):
        return jnp.concatenate([total, jnp.broadcast_to(mark, (8, width))], axis=0)

    ins[0].wait()
    ins[1].wait()
    v_st[...] = v_in[...].astype(F32)
    first_f = (docT[...] == head_doc).astype(F32)
    last_f = (docT[...] == tail_doc).astype(F32)
    for h in range(heads):
        lane = pl.ds(h, length, stride=heads)
        spk = spk_in[lane, :].astype(F32)
        vals = v_st[lane, :].astype(BF16)
        vb[h] = vals
        tail_f[pl.ds(h * width, width), :] = mm((spk * last_f).astype(BF16), vals, 0, 0)
        kb[h] = (spk * thr).astype(BF16)
        scatter(h, tail_f, recv_f, 0)

    ins[2].wait()
    ins[3].wait()
    q_st[...] = q_in[...].astype(F32)
    cot_st[...] = cot_in[...].astype(F32)
    s_at = lax.broadcasted_iota(jnp.int32, (length, length), 0)
    t_at = lax.broadcasted_iota(jnp.int32, (length, length), 1)
    doc_s = jnp.concatenate([docT[...]] * (length // width), axis=1)
    mask[...] = ((t_at <= s_at) & (doc_s == doc_row)).astype(F32)
    for h in range(heads):
        lane = pl.ds(h, length, stride=heads)
        qf = q_st[lane, :]
        qb[h] = qf.astype(BF16)
        sc = (mm(qb[h], kb[h], 1, 1) * mask[...]).astype(BF16)
        scores[h] = sc
        base[h] = qf + mm(sc, vb[h], 1, 0)

    pltpu.make_async_remote_copy(
        src_ref=meta.at[pl.ds(0, row_n - 1)],
        dst_ref=meta.at[pl.ds(0, row_n - 1)],
        send_sem=meta_s,
        recv_sem=meta_r,
        device_id=in_row(lax.rem(pos + 1, row_n)),
        device_id_type=MESH,
    ).wait_recv()
    scatter_descriptor(recv_f, 0).wait_recv()
    run = recv_f[0]
    before = meta[0, 1:2, :]
    send_f[0] = jnp.zeros((pr, width), F32)
    for j in range(1, row_n):
        head_j, tail_j = meta[j, 0:1, :], meta[j, 1:2, :]
        send_f[j] = jnp.where(before == head_j, run, 0.0)
        run = recv_f[j] + jnp.where(before == tail_j, run, 0.0)
        before = tail_j
    zs_f[...] = with_mark(run, before)
    hops_f = [between_rows(k, zs_f, zr_f, k - 1, 0) for k in (1, 2)]
    for cp in hops_f:
        cp.start()
    for cp in hops_f:
        cp.wait_recv()
    z1, z2 = zr_f[0, 0:pr, :], zr_f[1, 0:pr, :]
    m1, m2 = zr_f[0, pr : pr + 1, :], zr_f[1, pr : pr + 1, :]
    for j in range(row_n):
        head_j = meta[j, 0:1, :]
        send_f[j] = (
            send_f[j] + jnp.where(m1 == head_j, z1, 0.0) + jnp.where(m2 == head_j, z2, 0.0)
        )
    gather(send_f, carr, 0)

    gain_term = jnp.zeros((1, width), F32)
    cross = jnp.zeros((1, width), F32)
    for h in range(heads):
        gather_wait_chips(carr, 0, h)
        if h == 0:
            gather_wait_partner(carr, 0)
        lane = pl.ds(h, length, stride=heads)
        state = (carr[pl.ds(h * width, width), :] * thr_col).astype(BF16)
        mixed = base[h] + first_f * mm(qb[h], state, 1, 0)
        ratio = lax.rsqrt(jnp.mean(mixed * mixed, axis=-1, keepdims=True) + 1e-06)
        normed = mixed * ratio
        cot = cot_st[lane, :]
        upstream = cot * gain
        g = (
            ratio * upstream - normed * (ratio * jnp.mean(normed * upstream, axis=-1, keepdims=True))
        ).astype(BF16)
        gb[h] = g
        tail_b[pl.ds(h * width, width), :] = mm((q_st[lane, :] * first_f).astype(BF16), g, 0, 0)
        scatter(h, tail_b, recv_b, 1)
        att_st[lane, :] = normed * gain
        gain_term = gain_term + jnp.sum(cot * normed, axis=0, keepdims=True)

    att_out[...] = att_st[...].astype(BF16)
    outs = [pltpu.make_async_copy(att_out, att_hbm, out_sem.at[0])]
    outs[0].start()
    for h in range(heads):
        lane = pl.ds(h, length, stride=heads)
        rows = pl.ds(h * width, width)
        cs = carr[rows, :]
        cross = cross + jnp.sum(jnp.transpose(tail_b[rows, :] * cs), axis=0, keepdims=True)
        state = (cs * thr_col).astype(BF16)
        g = gb[h]
        ds = (mm(g, vb[h], 1, 1) * mask[...]).astype(BF16)
        out_st[lane, :] = g.astype(F32) + mm(ds, kb[h], 1, 0) + first_f * mm(g, state, 1, 1)
        kg = mm(ds, qb[h], 0, 0)
        cross = cross + jnp.sum(spk_in[lane, :].astype(F32) * kg, axis=0, keepdims=True)
        vgrad[h] = mm(scores[h], g, 0, 0)

    def total_copy(buf, mine, stage, device):
        return pltpu.make_async_remote_copy(
            src_ref=buf.at[mine],
            dst_ref=buf.at[mine],
            send_sem=ar_s.at[stage],
            recv_sem=ar_r.at[stage],
            device_id=device,
            device_id_type=MESH,
        )

    def total_start(buf, count, mine, stage, device, value):
        buf[pl.ds(mine, 1)] = value.reshape(1, 8, width)

        def body(k, c):
            total_copy(buf, mine, stage, device(k)).start()
            return c

        lax.fori_loop(1, count, body, 0)

    def total_descriptor(buf, count, stage, device):
        part = buf.at[pl.ds(0, count - 1)]
        return pltpu.make_async_remote_copy(
            src_ref=part,
            dst_ref=part,
            send_sem=ar_s.at[stage],
            recv_sem=ar_r.at[stage],
            device_id=device(1),
            device_id_type=MESH,
        )

    def row_peer(k):
        return in_row(lax.rem(pos + k, row_n))

    partial = jnp.where(
        sub == 0, jnp.broadcast_to(cross, (8, width)), jnp.broadcast_to(gain_term, (8, width))
    )
    total_start(ar_x, row_n, pos, 0, row_peer, partial)
    qg_out[...] = out_st[...].astype(BF16)
    outs.append(pltpu.make_async_copy(qg_out, qg_hbm, out_sem.at[1]))
    outs[1].start()

    scatter_descriptor(recv_b, 1).wait_recv()
    run = recv_b[row_n - 1]
    after = meta[row_n - 1, 0:1, :]
    send_b[row_n - 1] = jnp.zeros((pr, width), F32)
    for j in range(row_n - 2, -1, -1):
        head_j, tail_j = meta[j, 0:1, :], meta[j, 1:2, :]
        send_b[j] = jnp.where(after == tail_j, run, 0.0)
        run = recv_b[j] + jnp.where(after == head_j, run, 0.0)
        after = head_j
    zs_b[...] = with_mark(run, after)
    hops_b = [between_rows(n_rows - k, zs_b, zr_b, k - 1, 1) for k in (1, 2)]
    for cp in hops_b:
        cp.start()

    total_descriptor(ar_x, row_n, 0, row_peer).wait_recv()
    total_start(ar_z, n_rows, my_row, 1, along_z, jnp.sum(ar_x[...], axis=0))

    for cp in hops_b:
        cp.wait_recv()
    z1, z2 = zr_b[0, 0:pr, :], zr_b[1, 0:pr, :]
    m1, m2 = zr_b[0, pr : pr + 1, :], zr_b[1, pr : pr + 1, :]
    for j in range(row_n):
        tail_j = meta[j, 1:2, :]
        send_b[j] = (
            send_b[j] + jnp.where(m1 == tail_j, z1, 0.0) + jnp.where(m2 == tail_j, z2, 0.0)
        )
    gather(send_b, retn, 1)

    total_descriptor(ar_z, n_rows, 1, along_z).wait_recv()
    by_row = jnp.sum(ar_z[...], axis=0)
    if n_head > 1:
        total_start(ar_y, n_head, my_y, 2, along_y, by_row)

    for h in range(heads):
        gather_wait_chips(retn, 1, h)
        if h == 0:
            gather_wait_partner(retn, 1)
        lane = pl.ds(h, length, stride=heads)
        state = retn[pl.ds(h * width, width), :].astype(BF16)
        out_st[lane, :] = vgrad[h] + last_f * mm(kb[h], state, 1, 0)
    vg_out[...] = out_st[...].astype(BF16)
    outs.append(pltpu.make_async_copy(vg_out, vg_hbm, out_sem.at[2]))
    outs[2].start()

    if n_head > 1:
        total_descriptor(ar_y, n_head, 2, along_y).wait_recv()
        by_row = jnp.sum(ar_y[...], axis=0)
    scale = 1.0 / math.sqrt(length * n_ctx * heads * n_head)
    grads_ref[...] = by_row * scale

    for cp in outs:
        cp.wait()
    pltpu.make_async_remote_copy(
        src_ref=meta.at[pl.ds(0, row_n - 1)],
        dst_ref=meta.at[pl.ds(0, row_n - 1)],
        send_sem=meta_s,
        recv_sem=meta_r,
        device_id=row_peer(1),
        device_id_type=MESH,
    ).wait_send()
    for way, recv, send in ((0, recv_f, send_f), (1, recv_b, send_b)):
        scatter_descriptor(recv, way).wait_send()
        pltpu.make_async_remote_copy(
            src_ref=send.at[pl.ds(0, row_n - 1)],
            dst_ref=send.at[pl.ds(0, row_n - 1)],
            send_sem=st3_s.at[way],
            recv_sem=st3_r.at[way, 0],
            device_id=row_peer(1),
            device_id_type=MESH,
        ).wait_send()
    for cp in hops_f + hops_b:
        cp.wait_send()
    total_descriptor(ar_x, row_n, 0, row_peer).wait_send()
    total_descriptor(ar_z, n_rows, 1, along_z).wait_send()
    if n_head > 1:
        total_descriptor(ar_y, n_head, 2, along_y).wait_send()


def on_device(n_ctx, n_head, queries, spikes, values, threshold, norm_gain, document_ids, cotangent):
    length, heads, width = queries.shape
    dims = (n_ctx, n_head, ROW, length, heads, width)
    n_rows = n_ctx // ROW
    pr = width // (ROW // 2)
    flat = (length * heads, width)
    state = (heads * width, width)
    vmem = pl.BlockSpec(memory_space=pltpu.VMEM)
    hbm = pl.BlockSpec(memory_space=pl.ANY)
    dma = pltpu.SemaphoreType.DMA
    one_way = [
        pltpu.VMEM(state, F32),
        pltpu.VMEM((ROW, pr, width), F32),
        pltpu.VMEM((ROW, pr, width), F32),
        pltpu.VMEM((pr + 8, width), F32),
        pltpu.VMEM((2, pr + 8, width), F32),
        pltpu.VMEM(state, F32),
    ]
    att, qg, vg, grads = pl.pallas_call(
        functools.partial(kernel, dims),
        out_shape=[jax.ShapeDtypeStruct(flat, BF16)] * 3 + [jax.ShapeDtypeStruct((8, width), F32)],
        in_specs=[vmem] * 3 + [hbm] * 4,
        out_specs=[hbm] * 3 + [vmem],
        scratch_shapes=[
            pltpu.VMEM(flat, BF16),
            pltpu.VMEM(flat, jnp.int32),
            pltpu.VMEM(flat, BF16),
            pltpu.VMEM(flat, BF16),
            pltpu.VMEM(flat, F32),
            pltpu.VMEM(flat, F32),
            pltpu.VMEM(flat, F32),
            pltpu.VMEM((length, width), F32),
            pltpu.VMEM((length, length), F32),
            pltpu.VMEM((heads, length, width), BF16),
            pltpu.VMEM((heads, length, width), BF16),
            pltpu.VMEM((heads, length, width), BF16),
            pltpu.VMEM((heads, length, width), BF16),
            pltpu.VMEM((heads, length, length), BF16),
            pltpu.VMEM((heads, length, width), F32),
            pltpu.VMEM((heads, length, width), F32),
            pltpu.VMEM((8, width), F32),
            pltpu.VMEM((ROW, 8, width), F32),
            *one_way,
            *one_way,
            pltpu.VMEM(flat, F32),
            pltpu.VMEM(flat, F32),
            pltpu.VMEM((ROW, 8, width), F32),
            pltpu.VMEM((n_rows, 8, width), F32),
            pltpu.VMEM((max(n_head, 2), 8, width), F32),
            pltpu.VMEM(flat, BF16),
            pltpu.VMEM(flat, BF16),
            pltpu.VMEM(flat, BF16),
            dma((4,)),
            dma((3,)),
            dma,
            dma,
            dma((2,)),
            dma((2,)),
            dma((2, 2)),
            dma((2, 2)),
            dma((2,)),
            dma((2, 2)),
            dma((2,)),
            dma((3,)),
            dma((3,)),
        ],
        compiler_params=pltpu.CompilerParams(collective_id=0, has_side_effects=True),
    )(
        document_ids.reshape(1, length),
        threshold.reshape(1, width),
        norm_gain.reshape(1, width),
        queries.reshape(flat),
        spikes.reshape(flat),
        values.reshape(flat),
        cotangent.reshape(flat),
    )
    whole = (length, heads, width)
    return att.reshape(whole), qg.reshape(whole), vg.reshape(whole), grads[0], grads[1]


def solution(mesh):
    tokens = P("ctx", "head", None)
    return jax.shard_map(
        functools.partial(on_device, mesh.shape["ctx"], mesh.shape["head"]),
        mesh=mesh,
        in_specs=(tokens, tokens, tokens, P(), P(), P("ctx"), tokens),
        out_specs=(tokens, tokens, tokens, P(), P()),
        check_vma=False,
    )
```

```python
import functools
import math

import jax
import jax.numpy as jnp
from jax import lax
from jax.experimental import pallas as pl
from jax.experimental.pallas import tpu as pltpu
from jax.sharding import PartitionSpec as P

MESH = pl.DeviceIdType.MESH
F32 = jnp.float32
BF16 = jnp.bfloat16

ROW = 16


def mm(a, b, ca, cb):
    return lax.dot_general(a, b, (((ca,), (cb,)), ((), ())), preferred_element_type=F32)


def kernel(
    dims,
    docs_hbm,
    thr_hbm,
    gain_hbm,
    q_hbm,
    spk_hbm,
    v_hbm,
    cot_hbm,
    att_ref,
    qg_ref,
    vg_ref,
    grads_ref,
    docs_in,
    thr_in,
    gain_in,
    q_in,
    spk_in,
    v_in,
    cot_in,
    q_st,
    v_st,
    cot_st,
    docT,
    mask,
    qb,
    kb,
    vb,
    gb,
    scores,
    dscores,
    base,
    vgrad,
    meta_my,
    meta,
    tail_f,
    recv_f,
    send_f,
    zs_f,
    zr_f,
    carr,
    tail_b,
    recv_b,
    send_b,
    zs_b,
    zr_b,
    retn,
    att_st,
    out_st,
    ar_x,
    ar_z,
    ar_y,
    in_sem,
    meta_s,
    meta_r,
    st1_s,
    st1_r,
    st2_s,
    st2_r,
    st3_s,
    st3_r,
    st3_p,
    ar_s,
    ar_r,
    token,
    hello,
):
    n_ctx, n_head, row_n, length, heads, width = dims
    chips = row_n // 2
    n_rows = n_ctx // row_n
    pr = width // chips
    me = lax.axis_index("ctx")
    my_y = lax.axis_index("head")
    my_row = me // row_n
    row0 = my_row * row_n
    pos = me - row0
    my_chip = pos // 2
    my_core = pos - my_chip * 2
    mid = chips // 2

    def peer_chip(t):
        turn = (t + 1) // 2
        d = mid + turn * (1 - 2 * (t - 2 * (t // 2)))
        return lax.rem(my_chip + d, chips)

    def in_row(p):
        return {"ctx": row0 + p}

    def to_row(r):
        return {"ctx": r * row_n + pos}

    def along_z(k):
        return {"ctx": lax.rem(my_row + k, n_rows) * row_n + pos}

    def along_y(k):
        return {"head": lax.rem(my_y + k, n_head)}

    ins = [
        pltpu.make_async_copy(src, dst, in_sem.at[i])
        for i, (src, dst) in enumerate(
            (
                (docs_hbm, docs_in),
                (thr_hbm, thr_in),
                (spk_hbm, spk_in),
                (v_hbm, v_in),
                (q_hbm, q_in),
                (cot_hbm, cot_in),
                (gain_hbm, gain_in),
            )
        )
    ]
    for cp in ins:
        cp.start()

    barrier = pltpu.get_barrier_semaphore()

    def greet_row(k, c):
        pl.semaphore_signal(
            barrier, inc=1, device_id=in_row(lax.rem(pos + k, row_n)), device_id_type=MESH
        )
        return c

    def greet_y(k, c):
        pl.semaphore_signal(barrier, inc=1, device_id=along_y(k), device_id_type=MESH)
        return c

    lax.fori_loop(1, row_n, greet_row, 0)
    for k in (1, 2):

        @pl.when(my_row >= k)
        def _():
            pl.semaphore_signal(barrier, inc=1, device_id=to_row(my_row - k), device_id_type=MESH)

        @pl.when(my_row + k < n_rows)
        def _():
            pl.semaphore_signal(barrier, inc=1, device_id=to_row(my_row + k), device_id_type=MESH)

    if n_head > 1:
        lax.fori_loop(1, n_head, greet_y, 0)

    for k in range(2):

        @pl.when(my_row <= k)
        def _():
            zr_f[k] = jnp.full((pr + 8, width), -1.0, F32)

        @pl.when(my_row + k >= n_rows - 1)
        def _():
            zr_b[k] = jnp.full((pr + 8, width), -1.0, F32)

    ins[0].wait()
    ins[1].wait()
    doc_row = docs_in[...].astype(F32)
    docT[...] = jnp.transpose(jnp.broadcast_to(doc_row, (width, length)))
    head_doc = docT[0:1, :]
    tail_doc = docT[length - 1 : length, :]
    ends = jnp.concatenate([head_doc, tail_doc], axis=0)
    meta_my[...] = ends
    meta[pl.ds(pos, 1)] = ends.reshape(1, 2, width)
    thr = thr_in[...]
    thr_col = jnp.transpose(jnp.broadcast_to(thr, (width, width)))

    near = jnp.minimum(my_row, 2) + jnp.minimum(n_rows - 1 - my_row, 2)
    pl.semaphore_wait(barrier, (row_n - 1) + (n_head - 1) + near)

    def send_meta(t, c):
        chip = peer_chip(t)
        for core in range(2):
            pltpu.make_async_remote_copy(
                src_ref=meta_my,
                dst_ref=meta.at[pos],
                send_sem=meta_s,
                recv_sem=meta_r,
                device_id=in_row(chip * 2 + core),
                device_id_type=MESH,
            ).start()
        return c

    lax.fori_loop(0, chips - 1, send_meta, 0)
    pltpu.make_async_remote_copy(
        src_ref=meta_my,
        dst_ref=meta.at[pos],
        send_sem=meta_s,
        recv_sem=meta_r,
        device_id=in_row(my_chip * 2 + 1 - my_core),
        device_id_type=MESH,
    ).start()

    def scatter(h, tail, recv, way):
        def piece(chip):
            return tail.at[pl.ds(h * width + chip * pr, pr)]

        def one(chip):
            pltpu.make_async_remote_copy(
                src_ref=piece(chip),
                dst_ref=recv.at[pos],
                send_sem=st1_s.at[way],
                recv_sem=st1_r.at[way],
                device_id=in_row(chip * 2 + h),
                device_id_type=MESH,
            ).start()

        def body(t, c):
            one(peer_chip(t))
            return c

        lax.fori_loop(0, chips - 1, body, 0)

        @pl.when(my_core != h)
        def _():
            one(my_chip)

        @pl.when(my_core == h)
        def _():
            recv[pl.ds(pos, 1)] = tail[pl.ds(h * width + my_chip * pr, pr), :].reshape(
                1, pr, width
            )

    def scatter_descriptor(recv, way):
        return pltpu.make_async_remote_copy(
            src_ref=recv.at[pl.ds(0, row_n - 1)],
            dst_ref=recv.at[pl.ds(0, row_n - 1)],
            send_sem=st1_s.at[way],
            recv_sem=st1_r.at[way],
            device_id=in_row(lax.rem(pos + 1, row_n)),
            device_id_type=MESH,
        )

    def gather(send, land, way):
        at = my_core * width + my_chip * pr

        def one(p, rsem):
            pltpu.make_async_remote_copy(
                src_ref=send.at[p],
                dst_ref=land.at[pl.ds(at, pr)],
                send_sem=st3_s.at[way],
                recv_sem=rsem,
                device_id=in_row(p),
                device_id_type=MESH,
            ).start()

        def body(t, c):
            chip = peer_chip(t)
            for core in range(2):
                one(chip * 2 + core, st3_r.at[way, my_core])
            return c

        lax.fori_loop(0, chips - 1, body, 0)
        one(my_chip * 2 + 1 - my_core, st3_p.at[way])
        land[pl.ds(at, pr), :] = send[pl.ds(pos, 1)].reshape(pr, width)

    def gather_wait_chips(land, way, h):
        part = land.at[pl.ds(0, (chips - 1) * pr)]
        pltpu.make_async_remote_copy(
            src_ref=part,
            dst_ref=part,
            send_sem=st3_s.at[way],
            recv_sem=st3_r.at[way, h],
            device_id=in_row(lax.rem(pos + 1, row_n)),
            device_id_type=MESH,
        ).wait_recv()

    def gather_wait_partner(land, way):
        part = land.at[pl.ds(0, pr)]
        pltpu.make_async_remote_copy(
            src_ref=part,
            dst_ref=part,
            send_sem=st3_s.at[way],
            recv_sem=st3_p.at[way],
            device_id=in_row(lax.rem(pos + 1, row_n)),
            device_id_type=MESH,
        ).wait_recv()

    def row_hop(k, zs, zr, way):
        step = k * (1 - 2 * way)
        copy = pltpu.make_async_remote_copy(
            src_ref=zs,
            dst_ref=zr.at[k - 1],
            send_sem=st2_s.at[way, k - 1],
            recv_sem=st2_r.at[way, k - 1],
            device_id=to_row(my_row + step),
            device_id_type=MESH,
        )
        ahead = my_row + k < n_rows
        behind = my_row >= k
        return (copy, behind, ahead) if way else (copy, ahead, behind)

    def hops_start(hops):
        for copy, sends, _ in hops:
            pl.when(sends)(copy.start)

    def hops_wait_recv(hops):
        for copy, _, receives in hops:
            pl.when(receives)(copy.wait_recv)

    def hops_wait_send(hops):
        for copy, sends, _ in hops:
            pl.when(sends)(copy.wait_send)

    def with_mark(total, mark):
        return jnp.concatenate([total, jnp.broadcast_to(mark, (8, width))], axis=0)

    ins[2].wait()
    ins[3].wait()
    v_st[...] = v_in[...].astype(F32)
    first_f = (docT[...] == head_doc).astype(F32)
    last_f = (docT[...] == tail_doc).astype(F32)
    for h in range(heads):
        lane = pl.ds(h, length, stride=heads)
        spk = spk_in[lane, :].astype(F32)
        vals = v_st[lane, :].astype(BF16)
        vb[h] = vals
        tail_f[pl.ds(h * width, width), :] = mm((spk * last_f).astype(BF16), vals, 0, 0)
        kb[h] = (spk * thr).astype(BF16)
        scatter(h, tail_f, recv_f, 0)

    for cp in ins[4:]:
        cp.wait()
    gain = gain_in[...]
    q_st[...] = q_in[...].astype(F32)
    cot_st[...] = cot_in[...].astype(F32)
    s_at = lax.broadcasted_iota(jnp.int32, (length, length), 0)
    t_at = lax.broadcasted_iota(jnp.int32, (length, length), 1)
    doc_s = jnp.concatenate([docT[...]] * (length // width), axis=1)
    mask[...] = ((t_at <= s_at) & (doc_s == doc_row)).astype(F32)
    for h in range(heads):
        lane = pl.ds(h, length, stride=heads)
        qf = q_st[lane, :]
        qb[h] = qf.astype(BF16)
        sc = (mm(qb[h], kb[h], 1, 1) * mask[...]).astype(BF16)
        scores[h] = sc
        base[h] = qf + mm(sc, vb[h], 1, 0)

    pltpu.make_async_remote_copy(
        src_ref=meta.at[pl.ds(0, row_n - 1)],
        dst_ref=meta.at[pl.ds(0, row_n - 1)],
        send_sem=meta_s,
        recv_sem=meta_r,
        device_id=in_row(lax.rem(pos + 1, row_n)),
        device_id_type=MESH,
    ).wait_recv()
    scatter_descriptor(recv_f, 0).wait_recv()
    run = recv_f[0]
    before = meta[0, 1:2, :]
    send_f[0] = jnp.zeros((pr, width), F32)
    for j in range(1, row_n):
        head_j, tail_j = meta[j, 0:1, :], meta[j, 1:2, :]
        send_f[j] = jnp.where(before == head_j, run, 0.0)
        run = recv_f[j] + jnp.where(before == tail_j, run, 0.0)
        before = tail_j
    zs_f[...] = with_mark(run, before)
    hops_f = [row_hop(k, zs_f, zr_f, 0) for k in (1, 2)]
    hops_start(hops_f)
    hops_wait_recv(hops_f)
    z1, z2 = zr_f[0, 0:pr, :], zr_f[1, 0:pr, :]
    m1, m2 = zr_f[0, pr : pr + 1, :], zr_f[1, pr : pr + 1, :]
    for j in range(row_n):
        head_j = meta[j, 0:1, :]
        send_f[j] = (
            send_f[j] + jnp.where(m1 == head_j, z1, 0.0) + jnp.where(m2 == head_j, z2, 0.0)
        )
    gather(send_f, carr, 0)

    @pl.when(my_row > 0)
    def _():
        pl.semaphore_wait(token, 1)

    @pl.when(my_row < n_rows - 1)
    def _():
        pl.semaphore_signal(token, inc=1, device_id=to_row(my_row + 1), device_id_type=MESH)

    def greet_below(r, c):
        pl.semaphore_signal(hello, inc=1, device_id=to_row(r), device_id_type=MESH)
        return c

    lax.fori_loop(0, my_row, greet_below, 0)

    gain_term = jnp.zeros((1, width), F32)
    cross = jnp.zeros((1, width), F32)
    for h in range(heads):
        gather_wait_chips(carr, 0, h)
        if h == 0:
            gather_wait_partner(carr, 0)
        lane = pl.ds(h, length, stride=heads)
        state = (carr[pl.ds(h * width, width), :] * thr_col).astype(BF16)
        mixed = base[h] + first_f * mm(qb[h], state, 1, 0)
        ratio = lax.rsqrt(jnp.mean(mixed * mixed, axis=-1, keepdims=True) + 1e-06)
        normed = mixed * ratio
        cot = cot_st[lane, :]
        upstream = cot * gain
        g = (
            ratio * upstream - normed * (ratio * jnp.mean(normed * upstream, axis=-1, keepdims=True))
        ).astype(BF16)
        gb[h] = g
        tail_b[pl.ds(h * width, width), :] = mm((q_st[lane, :] * first_f).astype(BF16), g, 0, 0)
        att_st[lane, :] = normed * gain
        gain_term = gain_term + jnp.sum(cot * normed, axis=0, keepdims=True)

    def total_copy(buf, mine, stage, device):
        return pltpu.make_async_remote_copy(
            src_ref=buf.at[mine],
            dst_ref=buf.at[mine],
            send_sem=ar_s.at[stage],
            recv_sem=ar_r.at[stage],
            device_id=device,
            device_id_type=MESH,
        )

    def total_start(buf, count, mine, stage, device, value):
        buf[pl.ds(mine, 1)] = value.reshape(1, 2, width)

        def body(k, c):
            total_copy(buf, mine, stage, device(k)).start()
            return c

        lax.fori_loop(1, count, body, 0)

    def total_descriptor(buf, count, stage, device):
        part = buf.at[pl.ds(0, count - 1)]
        return pltpu.make_async_remote_copy(
            src_ref=part,
            dst_ref=part,
            send_sem=ar_s.at[stage],
            recv_sem=ar_r.at[stage],
            device_id=device(1),
            device_id_type=MESH,
        )

    def row_peer(k):
        return in_row(lax.rem(pos + k, row_n))

    for h in range(heads):
        lane = pl.ds(h, length, stride=heads)
        rows = pl.ds(h * width, width)
        cross = cross + jnp.sum(
            jnp.transpose(tail_b[rows, :] * carr[rows, :]), axis=0, keepdims=True
        )
        ds = (mm(gb[h], vb[h], 1, 1) * mask[...]).astype(BF16)
        dscores[h] = ds
        kg = mm(ds, qb[h], 0, 0)
        cross = cross + jnp.sum(spk_in[lane, :].astype(F32) * kg, axis=0, keepdims=True)
    total_start(ar_x, row_n, pos, 0, row_peer, jnp.concatenate([cross, gain_term], axis=0))

    for h in range(heads):
        scatter(h, tail_b, recv_b, 1)

    att_ref[...] = att_st[...].astype(BF16)
    for h in range(heads):
        lane = pl.ds(h, length, stride=heads)
        state = (carr[pl.ds(h * width, width), :] * thr_col).astype(BF16)
        g = gb[h]
        out_st[lane, :] = (
            g.astype(F32) + mm(dscores[h], kb[h], 1, 0) + first_f * mm(g, state, 1, 1)
        )
        vgrad[h] = mm(scores[h], g, 0, 0)
    qg_ref[...] = out_st[...].astype(BF16)

    total_descriptor(ar_x, row_n, 0, row_peer).wait_recv()
    total = jnp.sum(ar_x[...], axis=0)
    if n_head > 1:
        total_start(ar_y, n_head, my_y, 1, along_y, total)

    scatter_descriptor(recv_b, 1).wait_recv()
    run = recv_b[row_n - 1]
    after = meta[row_n - 1, 0:1, :]
    send_b[row_n - 1] = jnp.zeros((pr, width), F32)
    for j in range(row_n - 2, -1, -1):
        head_j, tail_j = meta[j, 0:1, :], meta[j, 1:2, :]
        send_b[j] = jnp.where(after == tail_j, run, 0.0)
        run = recv_b[j] + jnp.where(after == head_j, run, 0.0)
        after = head_j
    zs_b[...] = with_mark(run, after)
    hops_b = [row_hop(k, zs_b, zr_b, 1) for k in (1, 2)]
    hops_start(hops_b)

    if n_head > 1:
        total_descriptor(ar_y, n_head, 1, along_y).wait_recv()
        total = jnp.sum(ar_y[...], axis=0)

    @pl.when(my_row < n_rows - 1)
    def _():
        pl.semaphore_wait(hello, n_rows - 1 - my_row)

    total_start(ar_z, n_rows, my_row, 2, along_z, total)

    hops_wait_recv(hops_b)
    z1, z2 = zr_b[0, 0:pr, :], zr_b[1, 0:pr, :]
    m1, m2 = zr_b[0, pr : pr + 1, :], zr_b[1, pr : pr + 1, :]
    for j in range(row_n):
        tail_j = meta[j, 1:2, :]
        send_b[j] = (
            send_b[j] + jnp.where(m1 == tail_j, z1, 0.0) + jnp.where(m2 == tail_j, z2, 0.0)
        )
    gather(send_b, retn, 1)

    for h in range(heads):
        gather_wait_chips(retn, 1, h)
        if h == 0:
            gather_wait_partner(retn, 1)
        lane = pl.ds(h, length, stride=heads)
        state = retn[pl.ds(h * width, width), :].astype(BF16)
        out_st[lane, :] = vgrad[h] + last_f * mm(kb[h], state, 1, 0)
    vg_ref[...] = out_st[...].astype(BF16)

    total_descriptor(ar_z, n_rows, 2, along_z).wait_recv()
    scale = 1.0 / math.sqrt(length * n_ctx * heads * n_head)
    grads_ref[...] = jnp.sum(ar_z[...], axis=0) * scale

    pltpu.make_async_remote_copy(
        src_ref=meta.at[pl.ds(0, row_n - 1)],
        dst_ref=meta.at[pl.ds(0, row_n - 1)],
        send_sem=meta_s,
        recv_sem=meta_r,
        device_id=row_peer(1),
        device_id_type=MESH,
    ).wait_send()
    for way, recv, send in ((0, recv_f, send_f), (1, recv_b, send_b)):
        scatter_descriptor(recv, way).wait_send()
        pltpu.make_async_remote_copy(
            src_ref=send.at[pl.ds(0, row_n - 1)],
            dst_ref=send.at[pl.ds(0, row_n - 1)],
            send_sem=st3_s.at[way],
            recv_sem=st3_r.at[way, 0],
            device_id=row_peer(1),
            device_id_type=MESH,
        ).wait_send()
    hops_wait_send(hops_f + hops_b)
    total_descriptor(ar_x, row_n, 0, row_peer).wait_send()
    total_descriptor(ar_z, n_rows, 2, along_z).wait_send()
    if n_head > 1:
        total_descriptor(ar_y, n_head, 1, along_y).wait_send()


def put_out(att, qg, vg, grads, att_hbm, qg_hbm, vg_hbm, thr_hbm, gain_hbm, sem):
    pairs = (
        (att, att_hbm),
        (qg, qg_hbm),
        (vg, vg_hbm),
        (grads.at[pl.ds(0, 1)], thr_hbm),
        (grads.at[pl.ds(1, 1)], gain_hbm),
    )
    copies = [pltpu.make_async_copy(src, dst, sem.at[i]) for i, (src, dst) in enumerate(pairs)]
    for copy in copies:
        copy.start()
    for copy in copies:
        copy.wait()


def on_device(n_ctx, n_head, queries, spikes, values, threshold, norm_gain, document_ids, cotangent):
    length, heads, width = queries.shape
    dims = (n_ctx, n_head, ROW, length, heads, width)
    n_rows = n_ctx // ROW
    pr = width // (ROW // 2)
    flat = (length * heads, width)
    state = (heads * width, width)
    vmem = pl.BlockSpec(memory_space=pltpu.VMEM)
    hbm = pl.BlockSpec(memory_space=pl.ANY)
    dma = pltpu.SemaphoreType.DMA
    one_way = [
        pltpu.VMEM(state, F32),
        pltpu.VMEM((ROW, pr, width), F32),
        pltpu.VMEM((ROW, pr, width), F32),
        pltpu.VMEM((pr + 8, width), F32),
        pltpu.VMEM((2, pr + 8, width), F32),
        pltpu.VMEM(state, F32),
    ]
    results = pl.pallas_call(
        functools.partial(kernel, dims),
        out_shape=[pltpu.VMEM(flat, BF16)] * 3 + [pltpu.VMEM((2, width), F32)],
        in_specs=[hbm] * 7,
        out_specs=[vmem] * 4,
        scratch_shapes=[
            pltpu.VMEM((1, length), jnp.int32),
            pltpu.VMEM((1, width), F32),
            pltpu.VMEM((1, width), F32),
            pltpu.VMEM(flat, BF16),
            pltpu.VMEM(flat, jnp.int32),
            pltpu.VMEM(flat, BF16),
            pltpu.VMEM(flat, BF16),
            pltpu.VMEM(flat, F32),
            pltpu.VMEM(flat, F32),
            pltpu.VMEM(flat, F32),
            pltpu.VMEM((length, width), F32),
            pltpu.VMEM((length, length), F32),
            pltpu.VMEM((heads, length, width), BF16),
            pltpu.VMEM((heads, length, width), BF16),
            pltpu.VMEM((heads, length, width), BF16),
            pltpu.VMEM((heads, length, width), BF16),
            pltpu.VMEM((heads, length, length), BF16),
            pltpu.VMEM((heads, length, length), BF16),
            pltpu.VMEM((heads, length, width), F32),
            pltpu.VMEM((heads, length, width), F32),
            pltpu.VMEM((2, width), F32),
            pltpu.VMEM((ROW, 2, width), F32),
            *one_way,
            *one_way,
            pltpu.VMEM(flat, F32),
            pltpu.VMEM(flat, F32),
            pltpu.VMEM((ROW, 2, width), F32),
            pltpu.VMEM((n_rows, 2, width), F32),
            pltpu.VMEM((max(n_head, 2), 2, width), F32),
            dma((7,)),
            dma,
            dma,
            dma((2,)),
            dma((2,)),
            dma((2, 2)),
            dma((2, 2)),
            dma((2,)),
            dma((2, 2)),
            dma((2,)),
            dma((3,)),
            dma((3,)),
            pltpu.SemaphoreType.REGULAR,
            pltpu.SemaphoreType.REGULAR,
        ],
        compiler_params=pltpu.CompilerParams(collective_id=0, has_side_effects=True),
    )(
        document_ids.reshape(1, length),
        threshold.reshape(1, width),
        norm_gain.reshape(1, width),
        queries.reshape(flat),
        spikes.reshape(flat),
        values.reshape(flat),
        cotangent.reshape(flat),
    )
    att, qg, vg, thr_grad, gain_grad = pl.pallas_call(
        put_out,
        out_shape=[jax.ShapeDtypeStruct(flat, BF16)] * 3 + [jax.ShapeDtypeStruct((1, width), F32)] * 2,
        in_specs=[hbm] * 4,
        out_specs=[hbm] * 5,
        scratch_shapes=[dma((5,))],
        compiler_params=pltpu.CompilerParams(vmem_limit_bytes=1 << 20),
    )(*results)
    whole = (length, heads, width)
    return (
        att.reshape(whole),
        qg.reshape(whole),
        vg.reshape(whole),
        thr_grad.reshape(width),
        gain_grad.reshape(width),
    )


def solution(mesh):
    tokens = P("ctx", "head", None)
    return jax.shard_map(
        functools.partial(on_device, mesh.shape["ctx"], mesh.shape["head"]),
        mesh=mesh,
        in_specs=(tokens, tokens, tokens, P(), P(), P("ctx"), tokens),
        out_specs=(tokens, tokens, tokens, P(), P()),
        check_vma=False,
    )
```

```python
import functools
import math

import jax
import jax.numpy as jnp
from jax import lax
from jax.experimental import pallas as pl
from jax.experimental.pallas import tpu as pltpu
from jax.sharding import PartitionSpec as P

MESH = pl.DeviceIdType.MESH
F32 = jnp.float32
BF16 = jnp.bfloat16

ROW = 16


def mm(a, b, ca, cb):
    return lax.dot_general(a, b, (((ca,), (cb,)), ((), ())), preferred_element_type=F32)


def kernel(
    dims,
    docs_hbm,
    thr_hbm,
    gain_hbm,
    q_hbm,
    spk_hbm,
    v_hbm,
    cot_hbm,
    att_ref,
    qg_ref,
    vg_ref,
    grads_ref,
    docs_in,
    thr_in,
    gain_in,
    q_in,
    spk_in,
    v_in,
    cot_in,
    q_st,
    v_st,
    cot_st,
    docT,
    mask,
    qb,
    kb,
    vb,
    gb,
    qf1,
    cot_h,
    up_h,
    spk_h,
    att_h,
    ptail,
    chip_f,
    land,
    scores,
    dscores,
    base,
    vgrad,
    meta_my,
    meta,
    tail_f,
    recv_f,
    send_f,
    zs_f,
    zr_f,
    carr,
    tail_b,
    recv_b,
    send_b,
    zs_b,
    zr_b,
    retn,
    att_st,
    out_st,
    ar_x,
    ar_z,
    ar_y,
    in_sem,
    meta_s,
    meta_r,
    st1_s,
    st1_r,
    st2_s,
    st2_r,
    st3_s,
    st3_r,
    st3_p,
    ar_s,
    ar_r,
    token,
    hello,
    swap_s,
    swap_r,
):
    n_ctx, n_head, row_n, length, heads, width = dims
    chips = row_n // 2
    n_rows = n_ctx // row_n
    pr = width // chips
    me = lax.axis_index("ctx")
    my_y = lax.axis_index("head")
    my_row = me // row_n
    row0 = my_row * row_n
    pos = me - row0
    my_chip = pos // 2
    my_core = pos - my_chip * 2
    mid = chips // 2

    def peer_chip(t):
        turn = (t + 1) // 2
        d = mid + turn * (1 - 2 * (t - 2 * (t // 2)))
        return lax.rem(my_chip + d, chips)

    def in_row(p):
        return {"ctx": row0 + p}

    def row_peer(k):
        return in_row(lax.rem(pos + k, row_n))

    def to_row(r):
        return {"ctx": r * row_n + pos}

    def along_z(k):
        return {"ctx": lax.rem(my_row + k, n_rows) * row_n + pos}

    def along_y(k):
        return {"head": lax.rem(my_y + k, n_head)}

    ins = [
        pltpu.make_async_copy(src, dst, in_sem.at[i])
        for i, (src, dst) in enumerate(
            (
                (docs_hbm, docs_in),
                (thr_hbm, thr_in),
                (spk_hbm, spk_in),
                (v_hbm, v_in),
                (q_hbm, q_in),
                (cot_hbm, cot_in),
                (gain_hbm, gain_in),
            )
        )
    ]
    for cp in ins:
        cp.start()

    barrier = pltpu.get_barrier_semaphore()

    def greet_row(k, c):
        pl.semaphore_signal(
            barrier, inc=1, device_id=in_row(lax.rem(pos + k, row_n)), device_id_type=MESH
        )
        return c

    def greet_y(k, c):
        pl.semaphore_signal(barrier, inc=1, device_id=along_y(k), device_id_type=MESH)
        return c

    lax.fori_loop(1, row_n, greet_row, 0)
    for k in (1, 2):

        @pl.when(my_row >= k)
        def _():
            pl.semaphore_signal(barrier, inc=1, device_id=to_row(my_row - k), device_id_type=MESH)

        @pl.when(my_row + k < n_rows)
        def _():
            pl.semaphore_signal(barrier, inc=1, device_id=to_row(my_row + k), device_id_type=MESH)

    if n_head > 1:
        lax.fori_loop(1, n_head, greet_y, 0)

    for k in range(2):

        @pl.when(my_row <= k)
        def _():
            zr_f[k] = jnp.full((pr + 8, width), -1.0, F32)

        @pl.when(my_row + k >= n_rows - 1)
        def _():
            zr_b[k] = jnp.full((pr + 8, width), -1.0, F32)

    ins[0].wait()
    ins[1].wait()
    doc_row = docs_in[...].astype(F32)
    docT[...] = jnp.transpose(jnp.broadcast_to(doc_row, (width, length)))
    head_doc = docT[0:1, :]
    tail_doc = docT[length - 1 : length, :]
    ends = jnp.concatenate([head_doc, tail_doc], axis=0)
    meta_my[...] = ends
    meta[pl.ds(pos, 1)] = ends.reshape(1, 2, width)
    thr = thr_in[...]
    thr_col = jnp.transpose(jnp.broadcast_to(thr, (width, width)))

    near = jnp.minimum(my_row, 2) + jnp.minimum(n_rows - 1 - my_row, 2)
    pl.semaphore_wait(barrier, (row_n - 1) + (n_head - 1) + near)

    def send_meta(t, c):
        chip = peer_chip(t)
        for core in range(2):
            pltpu.make_async_remote_copy(
                src_ref=meta_my,
                dst_ref=meta.at[pos],
                send_sem=meta_s,
                recv_sem=meta_r,
                device_id=in_row(chip * 2 + core),
                device_id_type=MESH,
            ).start()
        return c

    lax.fori_loop(0, chips - 1, send_meta, 0)

    def to_partner(src, dst, i):
        return pltpu.make_async_remote_copy(
            src_ref=src,
            dst_ref=dst,
            send_sem=swap_s.at[i],
            recv_sem=swap_r.at[i],
            device_id=in_row(my_chip * 2 + 1 - my_core),
            device_id_type=MESH,
        )

    own_ends = to_partner(meta_my, meta.at[pos], 2)
    own_ends.start()

    def scatter(h, tail, recv, way):
        def piece(chip):
            return tail.at[pl.ds(h * width + chip * pr, pr)]

        def one(chip):
            pltpu.make_async_remote_copy(
                src_ref=piece(chip),
                dst_ref=recv.at[pos],
                send_sem=st1_s.at[way],
                recv_sem=st1_r.at[way],
                device_id=in_row(chip * 2 + h),
                device_id_type=MESH,
            ).start()

        def body(t, c):
            one(peer_chip(t))
            return c

        lax.fori_loop(0, chips - 1, body, 0)

        @pl.when(my_core != h)
        def _():
            one(my_chip)

        @pl.when(my_core == h)
        def _():
            recv[pl.ds(pos, 1)] = tail[pl.ds(h * width + my_chip * pr, pr), :].reshape(
                1, pr, width
            )

    def scatter_descriptor(recv, way):
        return pltpu.make_async_remote_copy(
            src_ref=recv.at[pl.ds(0, row_n - 1)],
            dst_ref=recv.at[pl.ds(0, row_n - 1)],
            send_sem=st1_s.at[way],
            recv_sem=st1_r.at[way],
            device_id=in_row(lax.rem(pos + 1, row_n)),
            device_id_type=MESH,
        )

    def gather(send, land, way):
        at = my_core * width + my_chip * pr

        def one(p, rsem):
            pltpu.make_async_remote_copy(
                src_ref=send.at[p],
                dst_ref=land.at[pl.ds(at, pr)],
                send_sem=st3_s.at[way],
                recv_sem=rsem,
                device_id=in_row(p),
                device_id_type=MESH,
            ).start()

        def body(t, c):
            chip = peer_chip(t)
            for core in range(2):
                one(chip * 2 + core, st3_r.at[way, my_core])
            return c

        lax.fori_loop(0, chips - 1, body, 0)
        one(my_chip * 2 + 1 - my_core, st3_p.at[way])
        land[pl.ds(at, pr), :] = send[pl.ds(pos, 1)].reshape(pr, width)

    def gather_wait_chips(land, way, h):
        part = land.at[pl.ds(0, (chips - 1) * pr)]
        pltpu.make_async_remote_copy(
            src_ref=part,
            dst_ref=part,
            send_sem=st3_s.at[way],
            recv_sem=st3_r.at[way, h],
            device_id=in_row(lax.rem(pos + 1, row_n)),
            device_id_type=MESH,
        ).wait_recv()

    def gather_wait_partner(land, way):
        part = land.at[pl.ds(0, pr)]
        pltpu.make_async_remote_copy(
            src_ref=part,
            dst_ref=part,
            send_sem=st3_s.at[way],
            recv_sem=st3_p.at[way],
            device_id=in_row(lax.rem(pos + 1, row_n)),
            device_id_type=MESH,
        ).wait_recv()

    def row_hop(k, zs, zr, way):
        step = k * (1 - 2 * way)
        copy = pltpu.make_async_remote_copy(
            src_ref=zs,
            dst_ref=zr.at[k - 1],
            send_sem=st2_s.at[way, k - 1],
            recv_sem=st2_r.at[way, k - 1],
            device_id=to_row(my_row + step),
            device_id_type=MESH,
        )
        ahead = my_row + k < n_rows
        behind = my_row >= k
        return (copy, behind, ahead) if way else (copy, ahead, behind)

    def hops_start(hops):
        for copy, sends, _ in hops:
            pl.when(sends)(copy.start)

    def hops_wait_recv(hops):
        for copy, _, receives in hops:
            pl.when(receives)(copy.wait_recv)

    def hops_wait_send(hops):
        for copy, sends, _ in hops:
            pl.when(sends)(copy.wait_send)

    def with_mark(total, mark):
        return jnp.concatenate([total, jnp.broadcast_to(mark, (8, width))], axis=0)

    ins[2].wait()
    ins[3].wait()
    v_st[...] = v_in[...].astype(F32)
    first_f = (docT[...] == head_doc).astype(F32)
    last_f = (docT[...] == tail_doc).astype(F32)
    for h in range(heads):
        lane = pl.ds(h, length, stride=heads)
        spk = spk_in[lane, :].astype(F32)
        vals = v_st[lane, :].astype(BF16)
        vb[h] = vals
        tail_f[pl.ds(h * width, width), :] = mm((spk * last_f).astype(BF16), vals, 0, 0)
        kb[h] = (spk * thr).astype(BF16)

    mine = pl.ds(pl.multiple_of(my_core * width, width), width)
    theirs = pl.ds(pl.multiple_of((1 - my_core) * width, width), width)
    for_theirs = to_partner(tail_f.at[theirs], ptail.at[theirs], 0)
    for_theirs.start()
    own_sums = to_partner(tail_f.at[mine], ptail.at[mine], 3)
    own_sums.start()
    own_ends.wait_recv()
    other = meta[pl.ds(my_chip * 2 + 1 - my_core, 1)].reshape(2, width)
    same_end = (other[1:2, :] == tail_doc).astype(F32)
    second = (my_core == 1).astype(F32)
    own_part = same_end + second * (1.0 - same_end)
    their_part = 1.0 + second * (same_end - 1.0)
    for_theirs.wait_recv()
    chip_f[...] = own_part * tail_f[mine, :] + their_part * ptail[mine, :]

    def chip_piece(t, c):
        chip = peer_chip(t)
        pltpu.make_async_remote_copy(
            src_ref=chip_f.at[pl.ds(chip * pr, pr)],
            dst_ref=recv_f.at[my_chip],
            send_sem=st1_s.at[0],
            recv_sem=st1_r.at[0],
            device_id=in_row(chip * 2 + my_core),
            device_id_type=MESH,
        ).start()
        return c

    lax.fori_loop(0, chips - 1, chip_piece, 0)
    recv_f[pl.ds(my_chip, 1)] = chip_f[pl.ds(my_chip * pr, pr), :].reshape(1, pr, width)
    pieces_f = pltpu.make_async_remote_copy(
        src_ref=recv_f.at[pl.ds(0, chips - 1)],
        dst_ref=recv_f.at[pl.ds(0, chips - 1)],
        send_sem=st1_s.at[0],
        recv_sem=st1_r.at[0],
        device_id=row_peer(1),
        device_id_type=MESH,
    )

    for cp in ins[4:]:
        cp.wait()
    gain = gain_in[...]
    q_st[...] = q_in[...].astype(F32)
    cot_st[...] = cot_in[...].astype(F32)
    s_at = lax.broadcasted_iota(jnp.int32, (length, length), 0)
    t_at = lax.broadcasted_iota(jnp.int32, (length, length), 1)
    doc_s = jnp.concatenate([docT[...]] * (length // width), axis=1)
    mask[...] = ((t_at <= s_at) & (doc_s == doc_row)).astype(F32)
    for h in range(heads):
        lane = pl.ds(h, length, stride=heads)
        qf = q_st[lane, :]
        qb[h] = qf.astype(BF16)
        qf1[h] = (qf * first_f).astype(BF16)
        cot = cot_st[lane, :]
        cot_h[h] = cot
        up_h[h] = cot * gain
        spk_h[h] = spk_in[lane, :].astype(F32)
        sc = (mm(qb[h], kb[h], 1, 1) * mask[...]).astype(BF16)
        scores[h] = sc
        base[h] = qf + mm(sc, vb[h], 1, 0)

    pltpu.make_async_remote_copy(
        src_ref=meta.at[pl.ds(0, row_n - 2)],
        dst_ref=meta.at[pl.ds(0, row_n - 2)],
        send_sem=meta_s,
        recv_sem=meta_r,
        device_id=in_row(lax.rem(pos + 1, row_n)),
        device_id_type=MESH,
    ).wait_recv()
    pieces_f.wait_recv()
    row_end = meta[row_n - 1, 1:2, :]
    run = recv_f[chips - 1]
    for j in range(chips - 1):
        run = run + jnp.where(meta[2 * j + 1, 1:2, :] == row_end, recv_f[j], 0.0)
    zs_f[...] = with_mark(run, row_end)
    hops_f = [row_hop(k, zs_f, zr_f, 0) for k in (1, 2)]
    hops_start(hops_f)
    run = recv_f[0]
    before = meta[1, 1:2, :]
    send_f[0] = jnp.zeros((pr, width), F32)
    for j in range(1, chips):
        head_j, tail_j = meta[2 * j, 0:1, :], meta[2 * j + 1, 1:2, :]
        send_f[j] = jnp.where(before == head_j, run, 0.0)
        run = recv_f[j] + jnp.where(before == tail_j, run, 0.0)
        before = tail_j
    hops_wait_recv(hops_f)
    z1, z2 = zr_f[0, 0:pr, :], zr_f[1, 0:pr, :]
    m1, m2 = zr_f[0, pr : pr + 1, :], zr_f[1, pr : pr + 1, :]
    for j in range(chips):
        head_j = meta[2 * j, 0:1, :]
        send_f[j] = (
            send_f[j] + jnp.where(m1 == head_j, z1, 0.0) + jnp.where(m2 == head_j, z2, 0.0)
        )

    def enter_chip(t, c):
        chip = peer_chip(t)
        pltpu.make_async_remote_copy(
            src_ref=send_f.at[chip],
            dst_ref=land.at[my_core, pl.ds(my_chip * pr, pr)],
            send_sem=st3_s.at[0],
            recv_sem=st3_r.at[0, 0],
            device_id=in_row(chip * 2 + my_core),
            device_id_type=MESH,
        ).start()
        return c

    lax.fori_loop(0, chips - 1, enter_chip, 0)
    land[pl.ds(my_core, 1), pl.ds(my_chip * pr, pr), :] = send_f[pl.ds(my_chip, 1)]
    entered = pltpu.make_async_remote_copy(
        src_ref=send_f.at[pl.ds(0, chips - 1)],
        dst_ref=send_f.at[pl.ds(0, chips - 1)],
        send_sem=st3_s.at[0],
        recv_sem=st3_r.at[0, 0],
        device_id=row_peer(1),
        device_id_type=MESH,
    )

    @pl.when(my_row > 0)
    def _():
        pl.semaphore_wait(token, 1)

    @pl.when(my_row < n_rows - 1)
    def _():
        pl.semaphore_signal(token, inc=1, device_id=to_row(my_row + 1), device_id_type=MESH)

    def greet_below(r, c):
        pl.semaphore_signal(hello, inc=1, device_id=to_row(r), device_id_type=MESH)
        return c

    lax.fori_loop(0, my_row, greet_below, 0)

    own_sums.wait_recv()
    joins = (other[1:2, :] == head_doc).astype(F32)
    whole = (other[0:1, :] == other[1:2, :]).astype(F32)
    by_partner = joins * second
    by_entry = 1.0 + second * (joins * whole - 1.0)

    gain_term = jnp.zeros((1, width), F32)
    cross = jnp.zeros((1, width), F32)
    entered.wait_recv()
    swap = to_partner(land.at[my_core], land.at[my_core], 1)
    swap.start()
    for turn in range(2):
        h = my_core if turn == 0 else 1 - my_core
        rows = pl.ds(pl.multiple_of(h * width, width), width)
        if turn == 1:
            swap.wait_recv()
        cs = by_entry * land[h] + by_partner * ptail[rows, :]
        carr[rows, :] = cs
        state = (cs * thr_col).astype(BF16)
        mixed = base[h] + mm(qf1[h], state, 1, 0)
        ratio = lax.rsqrt(jnp.mean(mixed * mixed, axis=-1, keepdims=True) + 1e-06)
        normed = mixed * ratio
        upstream = up_h[h]
        g = (
            ratio * upstream - normed * (ratio * jnp.mean(normed * upstream, axis=-1, keepdims=True))
        ).astype(BF16)
        gb[h] = g
        tail = mm(qf1[h], g, 0, 0)
        tail_b[rows, :] = tail
        cross = cross + jnp.sum(jnp.transpose(tail * cs), axis=0, keepdims=True)
        ds = (mm(g, vb[h], 1, 1) * mask[...]).astype(BF16)
        dscores[h] = ds
        kg = mm(ds, qb[h], 0, 0)
        cross = cross + jnp.sum(spk_h[h] * kg, axis=0, keepdims=True)
        gain_term = gain_term + jnp.sum(cot_h[h] * normed, axis=0, keepdims=True)
        att_h[h] = normed * gain

    def total_copy(buf, mine, stage, device):
        return pltpu.make_async_remote_copy(
            src_ref=buf.at[mine],
            dst_ref=buf.at[mine],
            send_sem=ar_s.at[stage],
            recv_sem=ar_r.at[stage],
            device_id=device,
            device_id_type=MESH,
        )

    def total_start(buf, count, mine, stage, device, value):
        buf[pl.ds(mine, 1)] = value.reshape(1, 2, width)

        def body(t, c):
            k = count // 2 + ((t + 1) // 2) * (1 - 2 * (t - 2 * (t // 2)))
            total_copy(buf, mine, stage, device(k)).start()
            return c

        lax.fori_loop(0, count - 1, body, 0)

    def total_descriptor(buf, count, stage, device):
        part = buf.at[pl.ds(0, count - 1)]
        return pltpu.make_async_remote_copy(
            src_ref=part,
            dst_ref=part,
            send_sem=ar_s.at[stage],
            recv_sem=ar_r.at[stage],
            device_id=device(1),
            device_id_type=MESH,
        )

    total_start(ar_x, row_n, pos, 0, row_peer, jnp.concatenate([cross, gain_term], axis=0))

    for h in range(heads):
        scatter(h, tail_b, recv_b, 1)

    for h in range(heads):
        lane = pl.ds(h, length, stride=heads)
        att_st[lane, :] = att_h[h]
        state = (carr[pl.ds(h * width, width), :] * thr_col).astype(BF16)
        g = gb[h]
        out_st[lane, :] = (
            g.astype(F32) + mm(dscores[h], kb[h], 1, 0) + first_f * mm(g, state, 1, 1)
        )
        vgrad[h] = mm(scores[h], g, 0, 0)
    att_ref[...] = att_st[...].astype(BF16)
    qg_ref[...] = out_st[...].astype(BF16)

    total_descriptor(ar_x, row_n, 0, row_peer).wait_recv()
    total = jnp.sum(ar_x[...], axis=0)
    if n_head > 1:
        total_start(ar_y, n_head, my_y, 1, along_y, total)

    scatter_descriptor(recv_b, 1).wait_recv()
    run = recv_b[row_n - 1]
    after = meta[row_n - 1, 0:1, :]
    send_b[row_n - 1] = jnp.zeros((pr, width), F32)
    for j in range(row_n - 2, -1, -1):
        head_j, tail_j = meta[j, 0:1, :], meta[j, 1:2, :]
        send_b[j] = jnp.where(after == tail_j, run, 0.0)
        run = recv_b[j] + jnp.where(after == head_j, run, 0.0)
        after = head_j
    zs_b[...] = with_mark(run, after)
    hops_b = [row_hop(k, zs_b, zr_b, 1) for k in (1, 2)]
    hops_start(hops_b)

    if n_head > 1:
        total_descriptor(ar_y, n_head, 1, along_y).wait_recv()
        total = jnp.sum(ar_y[...], axis=0)

    @pl.when(my_row < n_rows - 1)
    def _():
        pl.semaphore_wait(hello, n_rows - 1 - my_row)

    total_start(ar_z, n_rows, my_row, 2, along_z, total)

    hops_wait_recv(hops_b)
    z1, z2 = zr_b[0, 0:pr, :], zr_b[1, 0:pr, :]
    m1, m2 = zr_b[0, pr : pr + 1, :], zr_b[1, pr : pr + 1, :]
    for j in range(row_n):
        tail_j = meta[j, 1:2, :]
        send_b[j] = (
            send_b[j] + jnp.where(m1 == tail_j, z1, 0.0) + jnp.where(m2 == tail_j, z2, 0.0)
        )
    gather(send_b, retn, 1)

    for h in range(heads):
        gather_wait_chips(retn, 1, h)
        if h == 0:
            gather_wait_partner(retn, 1)
        lane = pl.ds(h, length, stride=heads)
        state = retn[pl.ds(h * width, width), :].astype(BF16)
        out_st[lane, :] = vgrad[h] + last_f * mm(kb[h], state, 1, 0)
    vg_ref[...] = out_st[...].astype(BF16)

    total_descriptor(ar_z, n_rows, 2, along_z).wait_recv()
    scale = 1.0 / math.sqrt(length * n_ctx * heads * n_head)
    grads_ref[...] = jnp.sum(ar_z[...], axis=0) * scale

    pltpu.make_async_remote_copy(
        src_ref=meta.at[pl.ds(0, row_n - 2)],
        dst_ref=meta.at[pl.ds(0, row_n - 2)],
        send_sem=meta_s,
        recv_sem=meta_r,
        device_id=row_peer(1),
        device_id_type=MESH,
    ).wait_send()
    pieces_f.wait_send()
    for_theirs.wait_send()
    own_ends.wait_send()
    scatter_descriptor(recv_b, 1).wait_send()
    own_sums.wait_send()
    entered.wait_send()
    swap.wait_send()
    pltpu.make_async_remote_copy(
        src_ref=send_b.at[pl.ds(0, row_n - 1)],
        dst_ref=send_b.at[pl.ds(0, row_n - 1)],
        send_sem=st3_s.at[1],
        recv_sem=st3_r.at[1, 0],
        device_id=row_peer(1),
        device_id_type=MESH,
    ).wait_send()
    hops_wait_send(hops_f + hops_b)
    total_descriptor(ar_x, row_n, 0, row_peer).wait_send()
    total_descriptor(ar_z, n_rows, 2, along_z).wait_send()
    if n_head > 1:
        total_descriptor(ar_y, n_head, 1, along_y).wait_send()


def put_out(att, qg, vg, grads, att_hbm, qg_hbm, vg_hbm, thr_hbm, gain_hbm, sem):
    pairs = (
        (att, att_hbm),
        (qg, qg_hbm),
        (vg, vg_hbm),
        (grads.at[pl.ds(0, 1)], thr_hbm),
        (grads.at[pl.ds(1, 1)], gain_hbm),
    )
    copies = [pltpu.make_async_copy(src, dst, sem.at[i]) for i, (src, dst) in enumerate(pairs)]
    for copy in copies:
        copy.start()
    for copy in copies:
        copy.wait()


def on_device(n_ctx, n_head, queries, spikes, values, threshold, norm_gain, document_ids, cotangent):
    length, heads, width = queries.shape
    dims = (n_ctx, n_head, ROW, length, heads, width)
    n_rows = n_ctx // ROW
    pr = width // (ROW // 2)
    flat = (length * heads, width)
    state = (heads * width, width)
    vmem = pl.BlockSpec(memory_space=pltpu.VMEM)
    hbm = pl.BlockSpec(memory_space=pl.ANY)
    dma = pltpu.SemaphoreType.DMA
    one_way = [
        pltpu.VMEM(state, F32),
        pltpu.VMEM((ROW, pr, width), F32),
        pltpu.VMEM((ROW, pr, width), F32),
        pltpu.VMEM((pr + 8, width), F32),
        pltpu.VMEM((2, pr + 8, width), F32),
        pltpu.VMEM(state, F32),
    ]
    results = pl.pallas_call(
        functools.partial(kernel, dims),
        out_shape=[pltpu.VMEM(flat, BF16)] * 3 + [pltpu.VMEM((2, width), F32)],
        in_specs=[hbm] * 7,
        out_specs=[vmem] * 4,
        scratch_shapes=[
            pltpu.VMEM((1, length), jnp.int32),
            pltpu.VMEM((1, width), F32),
            pltpu.VMEM((1, width), F32),
            pltpu.VMEM(flat, BF16),
            pltpu.VMEM(flat, jnp.int32),
            pltpu.VMEM(flat, BF16),
            pltpu.VMEM(flat, BF16),
            pltpu.VMEM(flat, F32),
            pltpu.VMEM(flat, F32),
            pltpu.VMEM(flat, F32),
            pltpu.VMEM((length, width), F32),
            pltpu.VMEM((length, length), F32),
            pltpu.VMEM((heads, length, width), BF16),
            pltpu.VMEM((heads, length, width), BF16),
            pltpu.VMEM((heads, length, width), BF16),
            pltpu.VMEM((heads, length, width), BF16),
            pltpu.VMEM((heads, length, width), BF16),
            pltpu.VMEM((heads, length, width), F32),
            pltpu.VMEM((heads, length, width), F32),
            pltpu.VMEM((heads, length, width), F32),
            pltpu.VMEM((heads, length, width), F32),
            pltpu.VMEM(state, F32),
            pltpu.VMEM((width, width), F32),
            pltpu.VMEM((heads, width, width), F32),
            pltpu.VMEM((heads, length, length), BF16),
            pltpu.VMEM((heads, length, length), BF16),
            pltpu.VMEM((heads, length, width), F32),
            pltpu.VMEM((heads, length, width), F32),
            pltpu.VMEM((2, width), F32),
            pltpu.VMEM((ROW, 2, width), F32),
            *one_way,
            *one_way,
            pltpu.VMEM(flat, F32),
            pltpu.VMEM(flat, F32),
            pltpu.VMEM((ROW, 2, width), F32),
            pltpu.VMEM((n_rows, 2, width), F32),
            pltpu.VMEM((max(n_head, 2), 2, width), F32),
            dma((7,)),
            dma,
            dma,
            dma((2,)),
            dma((2,)),
            dma((2, 2)),
            dma((2, 2)),
            dma((2,)),
            dma((2, 2)),
            dma((2,)),
            dma((3,)),
            dma((3,)),
            pltpu.SemaphoreType.REGULAR,
            pltpu.SemaphoreType.REGULAR,
            dma((4,)),
            dma((4,)),
        ],
        compiler_params=pltpu.CompilerParams(collective_id=0, has_side_effects=True),
    )(
        document_ids.reshape(1, length),
        threshold.reshape(1, width),
        norm_gain.reshape(1, width),
        queries.reshape(flat),
        spikes.reshape(flat),
        values.reshape(flat),
        cotangent.reshape(flat),
    )
    att, qg, vg, thr_grad, gain_grad = pl.pallas_call(
        put_out,
        out_shape=[jax.ShapeDtypeStruct(flat, BF16)] * 3 + [jax.ShapeDtypeStruct((1, width), F32)] * 2,
        in_specs=[hbm] * 4,
        out_specs=[hbm] * 5,
        scratch_shapes=[dma((5,))],
        compiler_params=pltpu.CompilerParams(vmem_limit_bytes=1 << 20),
    )(*results)
    whole = (length, heads, width)
    return (
        att.reshape(whole),
        qg.reshape(whole),
        vg.reshape(whole),
        thr_grad.reshape(width),
        gain_grad.reshape(width),
    )


def solution(mesh):
    tokens = P("ctx", "head", None)
    return jax.shard_map(
        functools.partial(on_device, mesh.shape["ctx"], mesh.shape["head"]),
        mesh=mesh,
        in_specs=(tokens, tokens, tokens, P(), P(), P("ctx"), tokens),
        out_specs=(tokens, tokens, tokens, P(), P()),
        check_vma=False,
    )
```

```python
import functools
import math

import jax
import jax.numpy as jnp
from jax import lax
from jax.experimental import pallas as pl
from jax.experimental.pallas import tpu as pltpu
from jax.sharding import PartitionSpec as P

MESH = pl.DeviceIdType.MESH
F32 = jnp.float32
BF16 = jnp.bfloat16

ROW = 16


def mm(a, b, ca, cb):
    return lax.dot_general(a, b, (((ca,), (cb,)), ((), ())), preferred_element_type=F32)


def kernel(
    dims,
    docs_hbm,
    thr_hbm,
    gain_hbm,
    q_hbm,
    spk_hbm,
    v_hbm,
    cot_hbm,
    att_ref,
    qg_ref,
    vg_ref,
    grads_ref,
    docs_in,
    thr_in,
    gain_in,
    q_in,
    spk_in,
    v_in,
    cot_in,
    q_st,
    v_st,
    cot_st,
    docT,
    mask,
    qb,
    kb,
    vb,
    gb,
    qf1,
    cot_h,
    up_h,
    q_h,
    back_h,
    sb,
    att_h,
    ptail,
    chip_f,
    land,
    scores,
    base,
    vgrad,
    meta_my,
    meta,
    tail_f,
    recv_f,
    send_f,
    zs_f,
    zr_f,
    tail_b,
    recv_b,
    send_b,
    zs_b,
    zr_b,
    retn,
    att_st,
    out_st,
    ar_x,
    ar_z,
    ar_y,
    in_sem,
    meta_s,
    meta_r,
    st1_s,
    st1_r,
    st2_s,
    st2_r,
    st3_s,
    st3_r,
    st3_p,
    ar_s,
    ar_r,
    token,
    hello,
    swap_s,
    swap_r,
):
    n_ctx, n_head, row_n, length, heads, width = dims
    chips = row_n // 2
    n_rows = n_ctx // row_n
    pr = width // chips
    me = lax.axis_index("ctx")
    my_y = lax.axis_index("head")
    my_row = me // row_n
    row0 = my_row * row_n
    pos = me - row0
    my_chip = pos // 2
    my_core = pos - my_chip * 2
    mid = chips // 2

    def peer_chip(t):
        turn = (t + 1) // 2
        d = mid + turn * (1 - 2 * (t - 2 * (t // 2)))
        return lax.rem(my_chip + d, chips)

    def in_row(p):
        return {"ctx": row0 + p}

    def row_peer(k):
        return in_row(lax.rem(pos + k, row_n))

    def to_row(r):
        return {"ctx": r * row_n + pos}

    def along_z(k):
        return {"ctx": lax.rem(my_row + k, n_rows) * row_n + pos}

    def along_y(k):
        return {"head": lax.rem(my_y + k, n_head)}

    ins = [
        pltpu.make_async_copy(src, dst, in_sem.at[i])
        for i, (src, dst) in enumerate(
            (
                (docs_hbm, docs_in),
                (thr_hbm, thr_in),
                (spk_hbm, spk_in),
                (v_hbm, v_in),
                (q_hbm, q_in),
                (cot_hbm, cot_in),
                (gain_hbm, gain_in),
            )
        )
    ]
    for cp in ins:
        cp.start()

    barrier = pltpu.get_barrier_semaphore()

    def greet_row(k, c):
        pl.semaphore_signal(
            barrier, inc=1, device_id=in_row(lax.rem(pos + k, row_n)), device_id_type=MESH
        )
        return c

    def greet_y(k, c):
        pl.semaphore_signal(barrier, inc=1, device_id=along_y(k), device_id_type=MESH)
        return c

    lax.fori_loop(1, row_n, greet_row, 0)
    for k in (1, 2):

        @pl.when(my_row >= k)
        def _():
            pl.semaphore_signal(barrier, inc=1, device_id=to_row(my_row - k), device_id_type=MESH)

        @pl.when(my_row + k < n_rows)
        def _():
            pl.semaphore_signal(barrier, inc=1, device_id=to_row(my_row + k), device_id_type=MESH)

    if n_head > 1:
        lax.fori_loop(1, n_head, greet_y, 0)

    for k in range(2):

        @pl.when(my_row <= k)
        def _():
            zr_f[k] = jnp.full((pr + 8, width), -1.0, F32)

        @pl.when(my_row + k >= n_rows - 1)
        def _():
            zr_b[k] = jnp.full((pr + 8, width), -1.0, F32)

    ins[0].wait()
    ins[1].wait()
    doc_row = docs_in[...].astype(F32)
    docT[...] = jnp.transpose(jnp.broadcast_to(doc_row, (width, length)))
    head_doc = docT[0:1, :]
    tail_doc = docT[length - 1 : length, :]
    ends = jnp.concatenate([head_doc, tail_doc], axis=0)
    meta_my[...] = ends
    meta[pl.ds(pos, 1)] = ends.reshape(1, 2, width)
    thr = thr_in[...]
    thr_col = jnp.transpose(jnp.broadcast_to(thr, (width, width)))

    near = jnp.minimum(my_row, 2) + jnp.minimum(n_rows - 1 - my_row, 2)
    pl.semaphore_wait(barrier, (row_n - 1) + (n_head - 1) + near)

    def send_meta(t, c):
        chip = peer_chip(t)
        for core in range(2):
            pltpu.make_async_remote_copy(
                src_ref=meta_my,
                dst_ref=meta.at[pos],
                send_sem=meta_s,
                recv_sem=meta_r,
                device_id=in_row(chip * 2 + core),
                device_id_type=MESH,
            ).start()
        return c

    lax.fori_loop(0, chips - 1, send_meta, 0)

    def to_partner(src, dst, i):
        return pltpu.make_async_remote_copy(
            src_ref=src,
            dst_ref=dst,
            send_sem=swap_s.at[i],
            recv_sem=swap_r.at[i],
            device_id=in_row(my_chip * 2 + 1 - my_core),
            device_id_type=MESH,
        )

    own_ends = to_partner(meta_my, meta.at[pos], 2)
    own_ends.start()

    def scatter(h, tail, recv, way):
        def piece(chip):
            return tail.at[pl.ds(h * width + chip * pr, pr)]

        def one(chip):
            pltpu.make_async_remote_copy(
                src_ref=piece(chip),
                dst_ref=recv.at[pos],
                send_sem=st1_s.at[way],
                recv_sem=st1_r.at[way],
                device_id=in_row(chip * 2 + h),
                device_id_type=MESH,
            ).start()

        def body(t, c):
            one(peer_chip(t))
            return c

        lax.fori_loop(0, chips - 1, body, 0)

        @pl.when(my_core != h)
        def _():
            one(my_chip)

        @pl.when(my_core == h)
        def _():
            recv[pl.ds(pos, 1)] = tail[pl.ds(h * width + my_chip * pr, pr), :].reshape(
                1, pr, width
            )

    def scatter_descriptor(recv, way):
        return pltpu.make_async_remote_copy(
            src_ref=recv.at[pl.ds(0, row_n - 1)],
            dst_ref=recv.at[pl.ds(0, row_n - 1)],
            send_sem=st1_s.at[way],
            recv_sem=st1_r.at[way],
            device_id=in_row(lax.rem(pos + 1, row_n)),
            device_id_type=MESH,
        )

    def gather(send, land, way):
        at = my_core * width + my_chip * pr

        def one(p, rsem):
            pltpu.make_async_remote_copy(
                src_ref=send.at[p],
                dst_ref=land.at[pl.ds(at, pr)],
                send_sem=st3_s.at[way],
                recv_sem=rsem,
                device_id=in_row(p),
                device_id_type=MESH,
            ).start()

        def body(t, c):
            chip = peer_chip(t)
            for core in range(2):
                one(chip * 2 + core, st3_r.at[way, my_core])
            return c

        lax.fori_loop(0, chips - 1, body, 0)
        one(my_chip * 2 + 1 - my_core, st3_p.at[way])
        land[pl.ds(at, pr), :] = send[pl.ds(pos, 1)].reshape(pr, width)

    def gather_wait_chips(land, way, h):
        part = land.at[pl.ds(0, (chips - 1) * pr)]
        pltpu.make_async_remote_copy(
            src_ref=part,
            dst_ref=part,
            send_sem=st3_s.at[way],
            recv_sem=st3_r.at[way, h],
            device_id=in_row(lax.rem(pos + 1, row_n)),
            device_id_type=MESH,
        ).wait_recv()

    def gather_wait_partner(land, way):
        part = land.at[pl.ds(0, pr)]
        pltpu.make_async_remote_copy(
            src_ref=part,
            dst_ref=part,
            send_sem=st3_s.at[way],
            recv_sem=st3_p.at[way],
            device_id=in_row(lax.rem(pos + 1, row_n)),
            device_id_type=MESH,
        ).wait_recv()

    def row_hop(k, zs, zr, way):
        step = k * (1 - 2 * way)
        copy = pltpu.make_async_remote_copy(
            src_ref=zs,
            dst_ref=zr.at[k - 1],
            send_sem=st2_s.at[way, k - 1],
            recv_sem=st2_r.at[way, k - 1],
            device_id=to_row(my_row + step),
            device_id_type=MESH,
        )
        ahead = my_row + k < n_rows
        behind = my_row >= k
        return (copy, behind, ahead) if way else (copy, ahead, behind)

    def hops_start(hops):
        for copy, sends, _ in hops:
            pl.when(sends)(copy.start)

    def hops_wait_recv(hops):
        for copy, _, receives in hops:
            pl.when(receives)(copy.wait_recv)

    def hops_wait_send(hops):
        for copy, sends, _ in hops:
            pl.when(sends)(copy.wait_send)

    def with_mark(total, mark):
        return jnp.concatenate([total, jnp.broadcast_to(mark, (8, width))], axis=0)

    ins[2].wait()
    ins[3].wait()
    v_st[...] = v_in[...].astype(F32)
    first_f = (docT[...] == head_doc).astype(F32)
    last_f = (docT[...] == tail_doc).astype(F32)
    for h in range(heads):
        lane = pl.ds(h, length, stride=heads)
        spk = spk_in[lane, :].astype(F32)
        vals = v_st[lane, :].astype(BF16)
        vb[h] = vals
        tail_f[pl.ds(h * width, width), :] = mm((spk * last_f).astype(BF16), vals, 0, 0)
        sb[h] = spk.astype(BF16)
        kb[h] = (spk * thr).astype(BF16)

    mine = pl.ds(pl.multiple_of(my_core * width, width), width)
    theirs = pl.ds(pl.multiple_of((1 - my_core) * width, width), width)
    for_theirs = to_partner(tail_f.at[theirs], ptail.at[theirs], 0)
    for_theirs.start()
    own_sums = to_partner(tail_f.at[mine], ptail.at[mine], 3)
    own_sums.start()
    own_ends.wait_recv()
    other = meta[pl.ds(my_chip * 2 + 1 - my_core, 1)].reshape(2, width)
    same_end = (other[1:2, :] == tail_doc).astype(F32)
    second = (my_core == 1).astype(F32)
    own_part = same_end + second * (1.0 - same_end)
    their_part = 1.0 + second * (same_end - 1.0)
    for_theirs.wait_recv()
    chip_f[...] = own_part * tail_f[mine, :] + their_part * ptail[mine, :]

    def chip_piece(t, c):
        chip = peer_chip(t)
        pltpu.make_async_remote_copy(
            src_ref=chip_f.at[pl.ds(chip * pr, pr)],
            dst_ref=recv_f.at[my_chip],
            send_sem=st1_s.at[0],
            recv_sem=st1_r.at[0],
            device_id=in_row(chip * 2 + my_core),
            device_id_type=MESH,
        ).start()
        return c

    lax.fori_loop(0, chips - 1, chip_piece, 0)
    recv_f[pl.ds(my_chip, 1)] = chip_f[pl.ds(my_chip * pr, pr), :].reshape(1, pr, width)
    pieces_f = pltpu.make_async_remote_copy(
        src_ref=recv_f.at[pl.ds(0, chips - 1)],
        dst_ref=recv_f.at[pl.ds(0, chips - 1)],
        send_sem=st1_s.at[0],
        recv_sem=st1_r.at[0],
        device_id=row_peer(1),
        device_id_type=MESH,
    )

    for cp in ins[4:]:
        cp.wait()
    gain = gain_in[...]
    q_st[...] = q_in[...].astype(F32)
    cot_st[...] = cot_in[...].astype(F32)
    s_at = lax.broadcasted_iota(jnp.int32, (length, length), 0)
    t_at = lax.broadcasted_iota(jnp.int32, (length, length), 1)
    doc_s = jnp.concatenate([docT[...]] * (length // width), axis=1)
    mask[...] = ((t_at <= s_at) & (doc_s == doc_row)).astype(F32)
    for h in range(heads):
        lane = pl.ds(h, length, stride=heads)
        qf = q_st[lane, :]
        qb[h] = qf.astype(BF16)
        qf1[h] = (qf * first_f).astype(BF16)
        cot = cot_st[lane, :]
        cot_h[h] = cot
        up_h[h] = cot * gain
        q_h[h] = qf
        sc = (mm(qb[h], kb[h], 1, 1) * mask[...]).astype(BF16)
        scores[h] = sc
        base[h] = qf + mm(sc, vb[h], 1, 0)

    pltpu.make_async_remote_copy(
        src_ref=meta.at[pl.ds(0, row_n - 2)],
        dst_ref=meta.at[pl.ds(0, row_n - 2)],
        send_sem=meta_s,
        recv_sem=meta_r,
        device_id=in_row(lax.rem(pos + 1, row_n)),
        device_id_type=MESH,
    ).wait_recv()
    pieces_f.wait_recv()
    row_end = meta[row_n - 1, 1:2, :]
    run = recv_f[chips - 1]
    for j in range(chips - 1):
        run = run + jnp.where(meta[2 * j + 1, 1:2, :] == row_end, recv_f[j], 0.0)
    zs_f[...] = with_mark(run, row_end)
    hops_f = [row_hop(k, zs_f, zr_f, 0) for k in (1, 2)]
    hops_start(hops_f)
    run = recv_f[0]
    before = meta[1, 1:2, :]
    send_f[0] = jnp.zeros((pr, width), F32)
    for j in range(1, chips):
        head_j, tail_j = meta[2 * j, 0:1, :], meta[2 * j + 1, 1:2, :]
        send_f[j] = jnp.where(before == head_j, run, 0.0)
        run = recv_f[j] + jnp.where(before == tail_j, run, 0.0)
        before = tail_j
    hops_wait_recv(hops_f)
    z1, z2 = zr_f[0, 0:pr, :], zr_f[1, 0:pr, :]
    m1, m2 = zr_f[0, pr : pr + 1, :], zr_f[1, pr : pr + 1, :]
    for j in range(chips):
        head_j = meta[2 * j, 0:1, :]
        send_f[j] = (
            send_f[j] + jnp.where(m1 == head_j, z1, 0.0) + jnp.where(m2 == head_j, z2, 0.0)
        )

    def enter_chip(t, c):
        chip = peer_chip(t)
        pltpu.make_async_remote_copy(
            src_ref=send_f.at[chip],
            dst_ref=land.at[my_core, pl.ds(my_chip * pr, pr)],
            send_sem=st3_s.at[0],
            recv_sem=st3_r.at[0, 0],
            device_id=in_row(chip * 2 + my_core),
            device_id_type=MESH,
        ).start()
        return c

    lax.fori_loop(0, chips - 1, enter_chip, 0)
    land[pl.ds(my_core, 1), pl.ds(my_chip * pr, pr), :] = send_f[pl.ds(my_chip, 1)]
    entered = pltpu.make_async_remote_copy(
        src_ref=send_f.at[pl.ds(0, chips - 1)],
        dst_ref=send_f.at[pl.ds(0, chips - 1)],
        send_sem=st3_s.at[0],
        recv_sem=st3_r.at[0, 0],
        device_id=row_peer(1),
        device_id_type=MESH,
    )

    @pl.when(my_row > 0)
    def _():
        pl.semaphore_wait(token, 1)

    @pl.when(my_row < n_rows - 1)
    def _():
        pl.semaphore_signal(token, inc=1, device_id=to_row(my_row + 1), device_id_type=MESH)

    def greet_below(r, c):
        pl.semaphore_signal(hello, inc=1, device_id=to_row(r), device_id_type=MESH)
        return c

    lax.fori_loop(0, my_row, greet_below, 0)

    own_sums.wait_recv()
    joins = (other[1:2, :] == head_doc).astype(F32)
    whole = (other[0:1, :] == other[1:2, :]).astype(F32)
    by_partner = joins * second
    by_entry = 1.0 + second * (joins * whole - 1.0)

    gain_term = jnp.zeros((1, width), F32)
    cross = jnp.zeros((1, width), F32)
    entered.wait_recv()
    swap = to_partner(land.at[my_core], land.at[my_core], 1)
    swap.start()
    for turn in range(2):
        h = my_core if turn == 0 else 1 - my_core
        rows = pl.ds(pl.multiple_of(h * width, width), width)
        if turn == 1:
            swap.wait_recv()
        cs = by_entry * land[h] + by_partner * ptail[rows, :]
        mixed = base[h] + mm(qf1[h], (cs * thr_col).astype(BF16), 1, 0)
        upstream = up_h[h]
        power = jnp.mean(mixed * mixed, axis=-1, keepdims=True)
        along = jnp.mean(mixed * upstream, axis=-1, keepdims=True)
        ratio = lax.rsqrt(power + 1e-06)
        normed = mixed * ratio
        g = (ratio * upstream - normed * (ratio * (ratio * along))).astype(BF16)
        gb[h] = g
        ds = (mm(g, vb[h], 1, 1) * mask[...]).astype(BF16)
        back = mm(ds, sb[h], 1, 0) + first_f * mm(g, cs.astype(BF16), 1, 1)
        back_h[h] = back
        cross = cross + jnp.sum(q_h[h] * back, axis=0, keepdims=True)
        gain_term = gain_term + jnp.sum(cot_h[h] * normed, axis=0, keepdims=True)
        att_h[h] = normed * gain

    def total_copy(buf, mine, stage, device):
        return pltpu.make_async_remote_copy(
            src_ref=buf.at[mine],
            dst_ref=buf.at[mine],
            send_sem=ar_s.at[stage],
            recv_sem=ar_r.at[stage],
            device_id=device,
            device_id_type=MESH,
        )

    def total_start(buf, count, mine, stage, device, value):
        buf[pl.ds(mine, 1)] = value.reshape(1, 2, width)

        def body(t, c):
            k = count // 2 + ((t + 1) // 2) * (1 - 2 * (t - 2 * (t // 2)))
            total_copy(buf, mine, stage, device(k)).start()
            return c

        lax.fori_loop(0, count - 1, body, 0)

    def total_descriptor(buf, count, stage, device):
        part = buf.at[pl.ds(0, count - 1)]
        return pltpu.make_async_remote_copy(
            src_ref=part,
            dst_ref=part,
            send_sem=ar_s.at[stage],
            recv_sem=ar_r.at[stage],
            device_id=device(1),
            device_id_type=MESH,
        )

    total_start(ar_x, row_n, pos, 0, row_peer, jnp.concatenate([cross, gain_term], axis=0))

    for h in range(heads):
        tail_b[pl.ds(h * width, width), :] = mm(qf1[h], gb[h], 0, 0)
        scatter(h, tail_b, recv_b, 1)

    for h in range(heads):
        lane = pl.ds(h, length, stride=heads)
        att_st[lane, :] = att_h[h]
        g = gb[h]
        out_st[lane, :] = g.astype(F32) + thr * back_h[h]
        vgrad[h] = mm(scores[h], g, 0, 0)
    att_ref[...] = att_st[...].astype(BF16)
    qg_ref[...] = out_st[...].astype(BF16)

    total_descriptor(ar_x, row_n, 0, row_peer).wait_recv()
    total = jnp.sum(ar_x[...], axis=0)
    if n_head > 1:
        total_start(ar_y, n_head, my_y, 1, along_y, total)

    scatter_descriptor(recv_b, 1).wait_recv()
    run = recv_b[row_n - 1]
    after = meta[row_n - 1, 0:1, :]
    send_b[row_n - 1] = jnp.zeros((pr, width), F32)
    for j in range(row_n - 2, -1, -1):
        head_j, tail_j = meta[j, 0:1, :], meta[j, 1:2, :]
        send_b[j] = jnp.where(after == tail_j, run, 0.0)
        run = recv_b[j] + jnp.where(after == head_j, run, 0.0)
        after = head_j
    zs_b[...] = with_mark(run, after)
    hops_b = [row_hop(k, zs_b, zr_b, 1) for k in (1, 2)]
    hops_start(hops_b)

    if n_head > 1:
        total_descriptor(ar_y, n_head, 1, along_y).wait_recv()
        total = jnp.sum(ar_y[...], axis=0)

    @pl.when(my_row < n_rows - 1)
    def _():
        pl.semaphore_wait(hello, n_rows - 1 - my_row)

    total_start(ar_z, n_rows, my_row, 2, along_z, total)

    hops_wait_recv(hops_b)
    z1, z2 = zr_b[0, 0:pr, :], zr_b[1, 0:pr, :]
    m1, m2 = zr_b[0, pr : pr + 1, :], zr_b[1, pr : pr + 1, :]
    for j in range(row_n):
        tail_j = meta[j, 1:2, :]
        send_b[j] = (
            send_b[j] + jnp.where(m1 == tail_j, z1, 0.0) + jnp.where(m2 == tail_j, z2, 0.0)
        )
    gather(send_b, retn, 1)

    for h in range(heads):
        gather_wait_chips(retn, 1, h)
        if h == 0:
            gather_wait_partner(retn, 1)
        lane = pl.ds(h, length, stride=heads)
        state = retn[pl.ds(h * width, width), :].astype(BF16)
        out_st[lane, :] = vgrad[h] + last_f * mm(kb[h], state, 1, 0)
    vg_ref[...] = out_st[...].astype(BF16)

    total_descriptor(ar_z, n_rows, 2, along_z).wait_recv()
    scale = 1.0 / math.sqrt(length * n_ctx * heads * n_head)
    grads_ref[...] = jnp.sum(ar_z[...], axis=0) * scale

    pltpu.make_async_remote_copy(
        src_ref=meta.at[pl.ds(0, row_n - 2)],
        dst_ref=meta.at[pl.ds(0, row_n - 2)],
        send_sem=meta_s,
        recv_sem=meta_r,
        device_id=row_peer(1),
        device_id_type=MESH,
    ).wait_send()
    pieces_f.wait_send()
    for_theirs.wait_send()
    own_ends.wait_send()
    scatter_descriptor(recv_b, 1).wait_send()
    own_sums.wait_send()
    entered.wait_send()
    swap.wait_send()
    pltpu.make_async_remote_copy(
        src_ref=send_b.at[pl.ds(0, row_n - 1)],
        dst_ref=send_b.at[pl.ds(0, row_n - 1)],
        send_sem=st3_s.at[1],
        recv_sem=st3_r.at[1, 0],
        device_id=row_peer(1),
        device_id_type=MESH,
    ).wait_send()
    hops_wait_send(hops_f + hops_b)
    total_descriptor(ar_x, row_n, 0, row_peer).wait_send()
    total_descriptor(ar_z, n_rows, 2, along_z).wait_send()
    if n_head > 1:
        total_descriptor(ar_y, n_head, 1, along_y).wait_send()


def put_out(att, qg, vg, grads, att_hbm, qg_hbm, vg_hbm, thr_hbm, gain_hbm, sem):
    pairs = (
        (att, att_hbm),
        (qg, qg_hbm),
        (vg, vg_hbm),
        (grads.at[pl.ds(0, 1)], thr_hbm),
        (grads.at[pl.ds(1, 1)], gain_hbm),
    )
    copies = [pltpu.make_async_copy(src, dst, sem.at[i]) for i, (src, dst) in enumerate(pairs)]
    for copy in copies:
        copy.start()
    for copy in copies:
        copy.wait()


def on_device(n_ctx, n_head, queries, spikes, values, threshold, norm_gain, document_ids, cotangent):
    length, heads, width = queries.shape
    dims = (n_ctx, n_head, ROW, length, heads, width)
    n_rows = n_ctx // ROW
    pr = width // (ROW // 2)
    flat = (length * heads, width)
    state = (heads * width, width)
    vmem = pl.BlockSpec(memory_space=pltpu.VMEM)
    hbm = pl.BlockSpec(memory_space=pl.ANY)
    dma = pltpu.SemaphoreType.DMA
    one_way = [
        pltpu.VMEM(state, F32),
        pltpu.VMEM((ROW, pr, width), F32),
        pltpu.VMEM((ROW, pr, width), F32),
        pltpu.VMEM((pr + 8, width), F32),
        pltpu.VMEM((2, pr + 8, width), F32),
        pltpu.VMEM(state, F32),
    ]
    results = pl.pallas_call(
        functools.partial(kernel, dims),
        out_shape=[pltpu.VMEM(flat, BF16)] * 3 + [pltpu.VMEM((2, width), F32)],
        in_specs=[hbm] * 7,
        out_specs=[vmem] * 4,
        scratch_shapes=[
            pltpu.VMEM((1, length), jnp.int32),
            pltpu.VMEM((1, width), F32),
            pltpu.VMEM((1, width), F32),
            pltpu.VMEM(flat, BF16),
            pltpu.VMEM(flat, jnp.int32),
            pltpu.VMEM(flat, BF16),
            pltpu.VMEM(flat, BF16),
            pltpu.VMEM(flat, F32),
            pltpu.VMEM(flat, F32),
            pltpu.VMEM(flat, F32),
            pltpu.VMEM((length, width), F32),
            pltpu.VMEM((length, length), F32),
            pltpu.VMEM((heads, length, width), BF16),
            pltpu.VMEM((heads, length, width), BF16),
            pltpu.VMEM((heads, length, width), BF16),
            pltpu.VMEM((heads, length, width), BF16),
            pltpu.VMEM((heads, length, width), BF16),
            pltpu.VMEM((heads, length, width), F32),
            pltpu.VMEM((heads, length, width), F32),
            pltpu.VMEM((heads, length, width), F32),
            pltpu.VMEM((heads, length, width), F32),
            pltpu.VMEM((heads, length, width), BF16),
            pltpu.VMEM((heads, length, width), F32),
            pltpu.VMEM(state, F32),
            pltpu.VMEM((width, width), F32),
            pltpu.VMEM((heads, width, width), F32),
            pltpu.VMEM((heads, length, length), BF16),
            pltpu.VMEM((heads, length, width), F32),
            pltpu.VMEM((heads, length, width), F32),
            pltpu.VMEM((2, width), F32),
            pltpu.VMEM((ROW, 2, width), F32),
            *one_way[:-1],
            *one_way,
            pltpu.VMEM(flat, F32),
            pltpu.VMEM(flat, F32),
            pltpu.VMEM((ROW, 2, width), F32),
            pltpu.VMEM((n_rows, 2, width), F32),
            pltpu.VMEM((max(n_head, 2), 2, width), F32),
            dma((7,)),
            dma,
            dma,
            dma((2,)),
            dma((2,)),
            dma((2, 2)),
            dma((2, 2)),
            dma((2,)),
            dma((2, 2)),
            dma((2,)),
            dma((3,)),
            dma((3,)),
            pltpu.SemaphoreType.REGULAR,
            pltpu.SemaphoreType.REGULAR,
            dma((4,)),
            dma((4,)),
        ],
        compiler_params=pltpu.CompilerParams(collective_id=0, has_side_effects=True),
    )(
        document_ids.reshape(1, length),
        threshold.reshape(1, width),
        norm_gain.reshape(1, width),
        queries.reshape(flat),
        spikes.reshape(flat),
        values.reshape(flat),
        cotangent.reshape(flat),
    )
    att, qg, vg, thr_grad, gain_grad = pl.pallas_call(
        put_out,
        out_shape=[jax.ShapeDtypeStruct(flat, BF16)] * 3 + [jax.ShapeDtypeStruct((1, width), F32)] * 2,
        in_specs=[hbm] * 4,
        out_specs=[hbm] * 5,
        scratch_shapes=[dma((5,))],
        compiler_params=pltpu.CompilerParams(vmem_limit_bytes=1 << 20),
    )(*results)
    whole = (length, heads, width)
    return (
        att.reshape(whole),
        qg.reshape(whole),
        vg.reshape(whole),
        thr_grad.reshape(width),
        gain_grad.reshape(width),
    )


def solution(mesh):
    tokens = P("ctx", "head", None)
    return jax.shard_map(
        functools.partial(on_device, mesh.shape["ctx"], mesh.shape["head"]),
        mesh=mesh,
        in_specs=(tokens, tokens, tokens, P(), P(), P("ctx"), tokens),
        out_specs=(tokens, tokens, tokens, P(), P()),
        check_vma=False,
    )
```

```python
import functools
import math

import jax
import jax.numpy as jnp
from jax import lax
from jax.experimental import pallas as pl
from jax.experimental.pallas import tpu as pltpu
from jax.sharding import PartitionSpec as P

MESH = pl.DeviceIdType.MESH
F32 = jnp.float32
BF16 = jnp.bfloat16

ROW = 16


def mm(a, b, ca, cb):
    return lax.dot_general(a, b, (((ca,), (cb,)), ((), ())), preferred_element_type=F32)


def kernel(
    dims,
    docs_hbm,
    thr_hbm,
    gain_hbm,
    q_hbm,
    spk_hbm,
    v_hbm,
    cot_hbm,
    att_ref,
    qg_ref,
    vg_ref,
    grads_ref,
    docs_in,
    thr_in,
    gain_in,
    q_in,
    spk_in,
    v_in,
    cot_in,
    q_st,
    v_st,
    cot_st,
    docT,
    mask,
    qb,
    kb,
    vb,
    gb,
    qf1,
    cot_h,
    up_h,
    q_h,
    back_h,
    sb,
    att_h,
    ptail,
    chip_f,
    land,
    scores,
    base,
    vgrad,
    meta_my,
    meta,
    tail_f,
    recv_f,
    send_f,
    zs_f,
    zr_f,
    tail_b,
    recv_b,
    send_b,
    zs_b,
    zr_b,
    retn,
    att_st,
    out_st,
    ar_x,
    ar_z,
    ar_y,
    in_sem,
    meta_s,
    meta_r,
    st1_s,
    st1_r,
    st2_s,
    st2_r,
    st3_s,
    st3_r,
    st3_p,
    ar_s,
    ar_r,
    token,
    hello,
    swap_s,
    swap_r,
):
    n_ctx, n_head, row_n, length, heads, width = dims
    chips = row_n // 2
    n_rows = n_ctx // row_n
    pr = width // chips
    me = lax.axis_index("ctx")
    my_y = lax.axis_index("head")
    my_row = me // row_n
    row0 = my_row * row_n
    pos = me - row0
    my_chip = pos // 2
    my_core = pos - my_chip * 2
    mid = chips // 2

    def peer_chip(t):
        turn = (t + 1) // 2
        d = mid + turn * (1 - 2 * (t - 2 * (t // 2)))
        return lax.rem(my_chip + d, chips)

    def in_row(p):
        return {"ctx": row0 + p}

    def row_peer(k):
        return in_row(lax.rem(pos + k, row_n))

    def to_row(r):
        return {"ctx": r * row_n + pos}

    def along_z(k):
        return {"ctx": lax.rem(my_row + k, n_rows) * row_n + pos}

    def along_y(k):
        return {"head": lax.rem(my_y + k, n_head)}

    ins = [
        pltpu.make_async_copy(src, dst, in_sem.at[i])
        for i, (src, dst) in enumerate(
            (
                (docs_hbm, docs_in),
                (thr_hbm, thr_in),
                (spk_hbm, spk_in),
                (v_hbm, v_in),
                (q_hbm, q_in),
                (cot_hbm, cot_in),
                (gain_hbm, gain_in),
            )
        )
    ]
    for cp in ins[:4]:
        cp.start()

    barrier = pltpu.get_barrier_semaphore()

    def greet_row(k, c):
        pl.semaphore_signal(
            barrier, inc=1, device_id=in_row(lax.rem(pos + k, row_n)), device_id_type=MESH
        )
        return c

    def greet_y(k, c):
        pl.semaphore_signal(barrier, inc=1, device_id=along_y(k), device_id_type=MESH)
        return c

    lax.fori_loop(1, row_n, greet_row, 0)
    for k in (1, 2):

        @pl.when(my_row >= k)
        def _():
            pl.semaphore_signal(barrier, inc=1, device_id=to_row(my_row - k), device_id_type=MESH)

        @pl.when(my_row + k < n_rows)
        def _():
            pl.semaphore_signal(barrier, inc=1, device_id=to_row(my_row + k), device_id_type=MESH)

    if n_head > 1:
        lax.fori_loop(1, n_head, greet_y, 0)

    for k in range(2):

        @pl.when(my_row <= k)
        def _():
            zr_f[k] = jnp.full((pr + 8, width), -1.0, F32)

        @pl.when(my_row + k >= n_rows - 1)
        def _():
            zr_b[k] = jnp.full((pr + 8, width), -1.0, F32)

    ins[0].wait()
    ins[1].wait()
    doc_row = docs_in[...].astype(F32)
    docT[...] = jnp.transpose(jnp.broadcast_to(doc_row, (width, length)))
    head_doc = docT[0:1, :]
    tail_doc = docT[length - 1 : length, :]
    ends = jnp.concatenate([head_doc, tail_doc], axis=0)
    meta_my[...] = ends
    meta[pl.ds(pos, 1)] = ends.reshape(1, 2, width)
    thr = thr_in[...]
    thr_col = jnp.transpose(jnp.broadcast_to(thr, (width, width)))

    near = jnp.minimum(my_row, 2) + jnp.minimum(n_rows - 1 - my_row, 2)
    pl.semaphore_wait(barrier, (row_n - 1) + (n_head - 1) + near)

    def send_meta(t, c):
        chip = peer_chip(t)
        for core in range(2):
            pltpu.make_async_remote_copy(
                src_ref=meta_my,
                dst_ref=meta.at[pos],
                send_sem=meta_s,
                recv_sem=meta_r,
                device_id=in_row(chip * 2 + core),
                device_id_type=MESH,
            ).start()
        return c

    lax.fori_loop(0, chips - 1, send_meta, 0)

    def to_partner(src, dst, i):
        return pltpu.make_async_remote_copy(
            src_ref=src,
            dst_ref=dst,
            send_sem=swap_s.at[i],
            recv_sem=swap_r.at[i],
            device_id=in_row(my_chip * 2 + 1 - my_core),
            device_id_type=MESH,
        )

    own_ends = to_partner(meta_my, meta.at[pos], 2)
    own_ends.start()

    def scatter(h, tail, recv, way):
        def piece(chip):
            return tail.at[pl.ds(h * width + chip * pr, pr)]

        def one(chip):
            pltpu.make_async_remote_copy(
                src_ref=piece(chip),
                dst_ref=recv.at[pos],
                send_sem=st1_s.at[way],
                recv_sem=st1_r.at[way],
                device_id=in_row(chip * 2 + h),
                device_id_type=MESH,
            ).start()

        def body(t, c):
            one(peer_chip(t))
            return c

        lax.fori_loop(0, chips - 1, body, 0)

        @pl.when(my_core != h)
        def _():
            one(my_chip)

        @pl.when(my_core == h)
        def _():
            recv[pl.ds(pos, 1)] = tail[pl.ds(h * width + my_chip * pr, pr), :].reshape(
                1, pr, width
            )

    def scatter_descriptor(recv, way):
        return pltpu.make_async_remote_copy(
            src_ref=recv.at[pl.ds(0, row_n - 1)],
            dst_ref=recv.at[pl.ds(0, row_n - 1)],
            send_sem=st1_s.at[way],
            recv_sem=st1_r.at[way],
            device_id=in_row(lax.rem(pos + 1, row_n)),
            device_id_type=MESH,
        )

    def gather(send, land, way):
        at = my_core * width + my_chip * pr

        def one(p, rsem):
            pltpu.make_async_remote_copy(
                src_ref=send.at[p],
                dst_ref=land.at[pl.ds(at, pr)],
                send_sem=st3_s.at[way],
                recv_sem=rsem,
                device_id=in_row(p),
                device_id_type=MESH,
            ).start()

        def body(t, c):
            chip = peer_chip(t)
            for core in range(2):
                one(chip * 2 + core, st3_r.at[way, my_core])
            return c

        lax.fori_loop(0, chips - 1, body, 0)
        one(my_chip * 2 + 1 - my_core, st3_p.at[way])
        land[pl.ds(at, pr), :] = send[pl.ds(pos, 1)].reshape(pr, width)

    def gather_wait_chips(land, way, h):
        part = land.at[pl.ds(0, (chips - 1) * pr)]
        pltpu.make_async_remote_copy(
            src_ref=part,
            dst_ref=part,
            send_sem=st3_s.at[way],
            recv_sem=st3_r.at[way, h],
            device_id=in_row(lax.rem(pos + 1, row_n)),
            device_id_type=MESH,
        ).wait_recv()

    def gather_wait_partner(land, way):
        part = land.at[pl.ds(0, pr)]
        pltpu.make_async_remote_copy(
            src_ref=part,
            dst_ref=part,
            send_sem=st3_s.at[way],
            recv_sem=st3_p.at[way],
            device_id=in_row(lax.rem(pos + 1, row_n)),
            device_id_type=MESH,
        ).wait_recv()

    def row_hop(k, zs, zr, way):
        step = k * (1 - 2 * way)
        copy = pltpu.make_async_remote_copy(
            src_ref=zs,
            dst_ref=zr.at[k - 1],
            send_sem=st2_s.at[way, k - 1],
            recv_sem=st2_r.at[way, k - 1],
            device_id=to_row(my_row + step),
            device_id_type=MESH,
        )
        ahead = my_row + k < n_rows
        behind = my_row >= k
        return (copy, behind, ahead) if way else (copy, ahead, behind)

    def hops_start(hops):
        for copy, sends, _ in hops:
            pl.when(sends)(copy.start)

    def hops_wait_recv(hops):
        for copy, _, receives in hops:
            pl.when(receives)(copy.wait_recv)

    def hops_wait_send(hops):
        for copy, sends, _ in hops:
            pl.when(sends)(copy.wait_send)

    def with_mark(total, mark):
        return jnp.concatenate([total, jnp.broadcast_to(mark, (8, width))], axis=0)

    for cp in ins[4:]:
        cp.start()
    ins[2].wait()
    ins[3].wait()
    v_st[...] = v_in[...].astype(F32)
    first_f = (docT[...] == head_doc).astype(F32)
    last_f = (docT[...] == tail_doc).astype(F32)
    for h in range(heads):
        lane = pl.ds(h, length, stride=heads)
        spk = spk_in[lane, :].astype(F32)
        vals = v_st[lane, :].astype(BF16)
        vb[h] = vals
        tail_f[pl.ds(h * width, width), :] = mm((spk * last_f).astype(BF16), vals, 0, 0)
        sb[h] = spk.astype(BF16)
        kb[h] = (spk * thr).astype(BF16)

    mine = pl.ds(pl.multiple_of(my_core * width, width), width)
    theirs = pl.ds(pl.multiple_of((1 - my_core) * width, width), width)
    for_theirs = to_partner(tail_f.at[theirs], ptail.at[theirs], 0)
    for_theirs.start()
    own_sums = to_partner(tail_f.at[mine], ptail.at[mine], 3)
    own_sums.start()
    own_ends.wait_recv()
    other = meta[pl.ds(my_chip * 2 + 1 - my_core, 1)].reshape(2, width)
    same_end = (other[1:2, :] == tail_doc).astype(F32)
    second = (my_core == 1).astype(F32)
    own_part = same_end + second * (1.0 - same_end)
    their_part = 1.0 + second * (same_end - 1.0)
    for_theirs.wait_recv()
    chip_f[...] = own_part * tail_f[mine, :] + their_part * ptail[mine, :]

    def chip_piece(t, c):
        chip = peer_chip(t)
        pltpu.make_async_remote_copy(
            src_ref=chip_f.at[pl.ds(chip * pr, pr)],
            dst_ref=recv_f.at[my_chip],
            send_sem=st1_s.at[0],
            recv_sem=st1_r.at[0],
            device_id=in_row(chip * 2 + my_core),
            device_id_type=MESH,
        ).start()
        return c

    lax.fori_loop(0, chips - 1, chip_piece, 0)
    recv_f[pl.ds(my_chip, 1)] = chip_f[pl.ds(my_chip * pr, pr), :].reshape(1, pr, width)
    pieces_f = pltpu.make_async_remote_copy(
        src_ref=recv_f.at[pl.ds(0, chips - 1)],
        dst_ref=recv_f.at[pl.ds(0, chips - 1)],
        send_sem=st1_s.at[0],
        recv_sem=st1_r.at[0],
        device_id=row_peer(1),
        device_id_type=MESH,
    )

    for cp in ins[4:]:
        cp.wait()
    gain = gain_in[...]
    q_st[...] = q_in[...].astype(F32)
    cot_st[...] = cot_in[...].astype(F32)
    s_at = lax.broadcasted_iota(jnp.int32, (length, length), 0)
    t_at = lax.broadcasted_iota(jnp.int32, (length, length), 1)
    doc_s = jnp.concatenate([docT[...]] * (length // width), axis=1)
    mask[...] = ((t_at <= s_at) & (doc_s == doc_row)).astype(F32)
    for h in range(heads):
        lane = pl.ds(h, length, stride=heads)
        qf = q_st[lane, :]
        qb[h] = qf.astype(BF16)
        qf1[h] = (qf * first_f).astype(BF16)
        cot = cot_st[lane, :]
        cot_h[h] = cot
        up_h[h] = cot * gain
        q_h[h] = qf
        sc = (mm(qb[h], kb[h], 1, 1) * mask[...]).astype(BF16)
        scores[h] = sc
        base[h] = qf + mm(sc, vb[h], 1, 0)

    pltpu.make_async_remote_copy(
        src_ref=meta.at[pl.ds(0, row_n - 2)],
        dst_ref=meta.at[pl.ds(0, row_n - 2)],
        send_sem=meta_s,
        recv_sem=meta_r,
        device_id=in_row(lax.rem(pos + 1, row_n)),
        device_id_type=MESH,
    ).wait_recv()
    pieces_f.wait_recv()
    row_end = meta[row_n - 1, 1:2, :]
    run = recv_f[chips - 1]
    for j in range(chips - 1):
        run = run + jnp.where(meta[2 * j + 1, 1:2, :] == row_end, recv_f[j], 0.0)
    zs_f[...] = with_mark(run, row_end)
    hops_f = [row_hop(k, zs_f, zr_f, 0) for k in (1, 2)]
    hops_start(hops_f)
    run = recv_f[0]
    before = meta[1, 1:2, :]
    send_f[0] = jnp.zeros((pr, width), F32)
    for j in range(1, chips):
        head_j, tail_j = meta[2 * j, 0:1, :], meta[2 * j + 1, 1:2, :]
        send_f[j] = jnp.where(before == head_j, run, 0.0)
        run = recv_f[j] + jnp.where(before == tail_j, run, 0.0)
        before = tail_j
    hops_wait_recv(hops_f)
    z1, z2 = zr_f[0, 0:pr, :], zr_f[1, 0:pr, :]
    m1, m2 = zr_f[0, pr : pr + 1, :], zr_f[1, pr : pr + 1, :]
    for j in range(chips):
        head_j = meta[2 * j, 0:1, :]
        send_f[j] = (
            send_f[j] + jnp.where(m1 == head_j, z1, 0.0) + jnp.where(m2 == head_j, z2, 0.0)
        )

    def enter_chip(t, c):
        chip = peer_chip(t)
        pltpu.make_async_remote_copy(
            src_ref=send_f.at[chip],
            dst_ref=land.at[my_core, pl.ds(my_chip * pr, pr)],
            send_sem=st3_s.at[0],
            recv_sem=st3_r.at[0, 0],
            device_id=in_row(chip * 2 + my_core),
            device_id_type=MESH,
        ).start()
        return c

    lax.fori_loop(0, chips - 1, enter_chip, 0)
    land[pl.ds(my_core, 1), pl.ds(my_chip * pr, pr), :] = send_f[pl.ds(my_chip, 1)]
    entered = pltpu.make_async_remote_copy(
        src_ref=send_f.at[pl.ds(0, chips - 1)],
        dst_ref=send_f.at[pl.ds(0, chips - 1)],
        send_sem=st3_s.at[0],
        recv_sem=st3_r.at[0, 0],
        device_id=row_peer(1),
        device_id_type=MESH,
    )

    @pl.when(my_row > 0)
    def _():
        pl.semaphore_wait(token, 1)

    @pl.when(my_row < n_rows - 1)
    def _():
        pl.semaphore_signal(token, inc=1, device_id=to_row(my_row + 1), device_id_type=MESH)

    def greet_below(r, c):
        pl.semaphore_signal(hello, inc=1, device_id=to_row(r), device_id_type=MESH)
        return c

    lax.fori_loop(0, my_row, greet_below, 0)

    own_sums.wait_recv()
    joins = (other[1:2, :] == head_doc).astype(F32)
    whole = (other[0:1, :] == other[1:2, :]).astype(F32)
    by_partner = joins * second
    by_entry = 1.0 + second * (joins * whole - 1.0)

    gain_term = jnp.zeros((1, width), F32)
    cross = jnp.zeros((1, width), F32)
    entered.wait_recv()
    swap = to_partner(land.at[my_core], land.at[my_core], 1)
    swap.start()
    for turn in range(2):
        h = my_core if turn == 0 else 1 - my_core
        rows = pl.ds(pl.multiple_of(h * width, width), width)
        if turn == 1:
            swap.wait_recv()
        cs = by_entry * land[h] + by_partner * ptail[rows, :]
        mixed = base[h] + mm(qf1[h], (cs * thr_col).astype(BF16), 1, 0)
        upstream = up_h[h]
        power = jnp.mean(mixed * mixed, axis=-1, keepdims=True)
        along = jnp.mean(mixed * upstream, axis=-1, keepdims=True)
        ratio = lax.rsqrt(power + 1e-06)
        normed = mixed * ratio
        g = (ratio * upstream - normed * (ratio * (ratio * along))).astype(BF16)
        gb[h] = g
        ds = (mm(g, vb[h], 1, 1) * mask[...]).astype(BF16)
        back = mm(ds, sb[h], 1, 0) + first_f * mm(g, cs.astype(BF16), 1, 1)
        back_h[h] = back
        cross = cross + jnp.sum(q_h[h] * back, axis=0, keepdims=True)
        gain_term = gain_term + jnp.sum(cot_h[h] * normed, axis=0, keepdims=True)
        att_h[h] = normed * gain

    def total_copy(buf, mine, stage, device):
        return pltpu.make_async_remote_copy(
            src_ref=buf.at[mine],
            dst_ref=buf.at[mine],
            send_sem=ar_s.at[stage],
            recv_sem=ar_r.at[stage],
            device_id=device,
            device_id_type=MESH,
        )

    def total_start(buf, count, mine, stage, device, value):
        buf[pl.ds(mine, 1)] = value.reshape(1, 2, width)

        def body(t, c):
            k = count // 2 + ((t + 1) // 2) * (1 - 2 * (t - 2 * (t // 2)))
            total_copy(buf, mine, stage, device(k)).start()
            return c

        lax.fori_loop(0, count - 1, body, 0)

    def total_descriptor(buf, count, stage, device):
        part = buf.at[pl.ds(0, count - 1)]
        return pltpu.make_async_remote_copy(
            src_ref=part,
            dst_ref=part,
            send_sem=ar_s.at[stage],
            recv_sem=ar_r.at[stage],
            device_id=device(1),
            device_id_type=MESH,
        )

    total_start(ar_x, row_n, pos, 0, row_peer, jnp.concatenate([cross, gain_term], axis=0))

    for h in range(heads):
        tail_b[pl.ds(h * width, width), :] = mm(qf1[h], gb[h], 0, 0)
        scatter(h, tail_b, recv_b, 1)

    for h in range(heads):
        lane = pl.ds(h, length, stride=heads)
        att_st[lane, :] = att_h[h]
        g = gb[h]
        out_st[lane, :] = g.astype(F32) + thr * back_h[h]
        vgrad[h] = mm(scores[h], g, 0, 0)
    att_ref[...] = att_st[...].astype(BF16)
    qg_ref[...] = out_st[...].astype(BF16)

    total_descriptor(ar_x, row_n, 0, row_peer).wait_recv()
    total = jnp.sum(ar_x[...], axis=0)
    if n_head > 1:
        total_start(ar_y, n_head, my_y, 1, along_y, total)

    scatter_descriptor(recv_b, 1).wait_recv()
    run = recv_b[row_n - 1]
    after = meta[row_n - 1, 0:1, :]
    send_b[row_n - 1] = jnp.zeros((pr, width), F32)
    for j in range(row_n - 2, -1, -1):
        head_j, tail_j = meta[j, 0:1, :], meta[j, 1:2, :]
        send_b[j] = jnp.where(after == tail_j, run, 0.0)
        run = recv_b[j] + jnp.where(after == head_j, run, 0.0)
        after = head_j
    zs_b[...] = with_mark(run, after)
    hops_b = [row_hop(k, zs_b, zr_b, 1) for k in (1, 2)]
    hops_start(hops_b)

    if n_head > 1:
        total_descriptor(ar_y, n_head, 1, along_y).wait_recv()
        total = jnp.sum(ar_y[...], axis=0)

    @pl.when(my_row < n_rows - 1)
    def _():
        pl.semaphore_wait(hello, n_rows - 1 - my_row)

    total_start(ar_z, n_rows, my_row, 2, along_z, total)

    hops_wait_recv(hops_b)
    z1, z2 = zr_b[0, 0:pr, :], zr_b[1, 0:pr, :]
    m1, m2 = zr_b[0, pr : pr + 1, :], zr_b[1, pr : pr + 1, :]
    for j in range(row_n):
        tail_j = meta[j, 1:2, :]
        send_b[j] = (
            send_b[j] + jnp.where(m1 == tail_j, z1, 0.0) + jnp.where(m2 == tail_j, z2, 0.0)
        )
    gather(send_b, retn, 1)

    for h in range(heads):
        gather_wait_chips(retn, 1, h)
        if h == 0:
            gather_wait_partner(retn, 1)
        lane = pl.ds(h, length, stride=heads)
        state = retn[pl.ds(h * width, width), :].astype(BF16)
        out_st[lane, :] = vgrad[h] + last_f * mm(kb[h], state, 1, 0)
    vg_ref[...] = out_st[...].astype(BF16)

    total_descriptor(ar_z, n_rows, 2, along_z).wait_recv()
    scale = 1.0 / math.sqrt(length * n_ctx * heads * n_head)
    grads_ref[...] = jnp.sum(ar_z[...], axis=0) * scale

    pltpu.make_async_remote_copy(
        src_ref=meta.at[pl.ds(0, row_n - 2)],
        dst_ref=meta.at[pl.ds(0, row_n - 2)],
        send_sem=meta_s,
        recv_sem=meta_r,
        device_id=row_peer(1),
        device_id_type=MESH,
    ).wait_send()
    pieces_f.wait_send()
    for_theirs.wait_send()
    own_ends.wait_send()
    scatter_descriptor(recv_b, 1).wait_send()
    own_sums.wait_send()
    entered.wait_send()
    swap.wait_send()
    pltpu.make_async_remote_copy(
        src_ref=send_b.at[pl.ds(0, row_n - 1)],
        dst_ref=send_b.at[pl.ds(0, row_n - 1)],
        send_sem=st3_s.at[1],
        recv_sem=st3_r.at[1, 0],
        device_id=row_peer(1),
        device_id_type=MESH,
    ).wait_send()
    hops_wait_send(hops_f + hops_b)
    total_descriptor(ar_x, row_n, 0, row_peer).wait_send()
    total_descriptor(ar_z, n_rows, 2, along_z).wait_send()
    if n_head > 1:
        total_descriptor(ar_y, n_head, 1, along_y).wait_send()


def put_out(att, qg, vg, grads, att_hbm, qg_hbm, vg_hbm, thr_hbm, gain_hbm, sem):
    pairs = [(grads.at[pl.ds(0, 1)], thr_hbm), (grads.at[pl.ds(1, 1)], gain_hbm)]
    half = att.shape[0] // 2
    for src, dst in ((att, att_hbm), (qg, qg_hbm), (vg, vg_hbm)):
        for part in range(2):
            rows = pl.ds(part * half, half)
            pairs.append((src.at[rows], dst.at[rows]))
    copies = [pltpu.make_async_copy(src, dst, sem.at[i]) for i, (src, dst) in enumerate(pairs)]
    for copy in copies:
        copy.start()
    for copy in copies:
        copy.wait()


def on_device(n_ctx, n_head, queries, spikes, values, threshold, norm_gain, document_ids, cotangent):
    length, heads, width = queries.shape
    dims = (n_ctx, n_head, ROW, length, heads, width)
    n_rows = n_ctx // ROW
    pr = width // (ROW // 2)
    flat = (length * heads, width)
    state = (heads * width, width)
    vmem = pl.BlockSpec(memory_space=pltpu.VMEM)
    hbm = pl.BlockSpec(memory_space=pl.ANY)
    dma = pltpu.SemaphoreType.DMA
    one_way = [
        pltpu.VMEM(state, F32),
        pltpu.VMEM((ROW, pr, width), F32),
        pltpu.VMEM((ROW, pr, width), F32),
        pltpu.VMEM((pr + 8, width), F32),
        pltpu.VMEM((2, pr + 8, width), F32),
        pltpu.VMEM(state, F32),
    ]
    results = pl.pallas_call(
        functools.partial(kernel, dims),
        out_shape=[pltpu.VMEM(flat, BF16)] * 3 + [pltpu.VMEM((2, width), F32)],
        in_specs=[hbm] * 7,
        out_specs=[vmem] * 4,
        scratch_shapes=[
            pltpu.VMEM((1, length), jnp.int32),
            pltpu.VMEM((1, width), F32),
            pltpu.VMEM((1, width), F32),
            pltpu.VMEM(flat, BF16),
            pltpu.VMEM(flat, jnp.int32),
            pltpu.VMEM(flat, BF16),
            pltpu.VMEM(flat, BF16),
            pltpu.VMEM(flat, F32),
            pltpu.VMEM(flat, F32),
            pltpu.VMEM(flat, F32),
            pltpu.VMEM((length, width), F32),
            pltpu.VMEM((length, length), F32),
            pltpu.VMEM((heads, length, width), BF16),
            pltpu.VMEM((heads, length, width), BF16),
            pltpu.VMEM((heads, length, width), BF16),
            pltpu.VMEM((heads, length, width), BF16),
            pltpu.VMEM((heads, length, width), BF16),
            pltpu.VMEM((heads, length, width), F32),
            pltpu.VMEM((heads, length, width), F32),
            pltpu.VMEM((heads, length, width), F32),
            pltpu.VMEM((heads, length, width), F32),
            pltpu.VMEM((heads, length, width), BF16),
            pltpu.VMEM((heads, length, width), F32),
            pltpu.VMEM(state, F32),
            pltpu.VMEM((width, width), F32),
            pltpu.VMEM((heads, width, width), F32),
            pltpu.VMEM((heads, length, length), BF16),
            pltpu.VMEM((heads, length, width), F32),
            pltpu.VMEM((heads, length, width), F32),
            pltpu.VMEM((2, width), F32),
            pltpu.VMEM((ROW, 2, width), F32),
            *one_way[:-1],
            *one_way,
            pltpu.VMEM(flat, F32),
            pltpu.VMEM(flat, F32),
            pltpu.VMEM((ROW, 2, width), F32),
            pltpu.VMEM((n_rows, 2, width), F32),
            pltpu.VMEM((max(n_head, 2), 2, width), F32),
            dma((7,)),
            dma,
            dma,
            dma((2,)),
            dma((2,)),
            dma((2, 2)),
            dma((2, 2)),
            dma((2,)),
            dma((2, 2)),
            dma((2,)),
            dma((3,)),
            dma((3,)),
            pltpu.SemaphoreType.REGULAR,
            pltpu.SemaphoreType.REGULAR,
            dma((4,)),
            dma((4,)),
        ],
        compiler_params=pltpu.CompilerParams(collective_id=0, has_side_effects=True),
    )(
        document_ids.reshape(1, length),
        threshold.reshape(1, width),
        norm_gain.reshape(1, width),
        queries.reshape(flat),
        spikes.reshape(flat),
        values.reshape(flat),
        cotangent.reshape(flat),
    )
    att, qg, vg, thr_grad, gain_grad = pl.pallas_call(
        put_out,
        out_shape=[jax.ShapeDtypeStruct(flat, BF16)] * 3 + [jax.ShapeDtypeStruct((1, width), F32)] * 2,
        in_specs=[hbm] * 4,
        out_specs=[hbm] * 5,
        scratch_shapes=[dma((8,))],
        compiler_params=pltpu.CompilerParams(vmem_limit_bytes=1 << 20),
    )(*results)
    whole = (length, heads, width)
    return (
        att.reshape(whole),
        qg.reshape(whole),
        vg.reshape(whole),
        thr_grad.reshape(width),
        gain_grad.reshape(width),
    )


def solution(mesh):
    tokens = P("ctx", "head", None)
    return jax.shard_map(
        functools.partial(on_device, mesh.shape["ctx"], mesh.shape["head"]),
        mesh=mesh,
        in_specs=(tokens, tokens, tokens, P(), P(), P("ctx"), tokens),
        out_specs=(tokens, tokens, tokens, P(), P()),
        check_vma=False,
    )
```

```python
import functools
import math

import jax
import jax.numpy as jnp
from jax import lax
from jax.experimental import pallas as pl
from jax.experimental.pallas import tpu as pltpu
from jax.sharding import PartitionSpec as P

MESH = pl.DeviceIdType.MESH
F32 = jnp.float32
BF16 = jnp.bfloat16

ROW = 16


def mm(a, b, ca, cb):
    return lax.dot_general(a, b, (((ca,), (cb,)), ((), ())), preferred_element_type=F32)


def kernel(
    dims,
    docs_hbm,
    thr_hbm,
    gain_hbm,
    q_hbm,
    spk_hbm,
    v_hbm,
    cot_hbm,
    att_ref,
    qg_ref,
    vg_ref,
    grads_ref,
    docs_in,
    thr_in,
    gain_in,
    q_in,
    spk_in,
    v_in,
    cot_in,
    q_st,
    v_st,
    cot_st,
    docT,
    mask,
    qb,
    kb,
    vb,
    gb,
    qf1,
    cot_h,
    up_h,
    q_h,
    back_h,
    sb,
    att_h,
    ptail,
    chip_f,
    land,
    scores,
    base,
    vgrad,
    meta_my,
    meta,
    tail_f,
    recv_f,
    send_f,
    zs_f,
    zr_f,
    tail_b,
    recv_b,
    send_b,
    zs_b,
    zr_b,
    retn,
    att_st,
    out_st,
    ar_x,
    ar_z,
    ar_y,
    in_sem,
    meta_s,
    meta_r,
    st1_s,
    st1_r,
    st2_s,
    st2_r,
    st3_s,
    st3_r,
    st3_p,
    ar_s,
    ar_r,
    token,
    hello,
    swap_s,
    swap_r,
):
    n_ctx, n_head, row_n, length, heads, width = dims
    chips = row_n // 2
    n_rows = n_ctx // row_n
    pr = width // chips
    me = lax.axis_index("ctx")
    my_y = lax.axis_index("head")
    my_row = me // row_n
    row0 = my_row * row_n
    pos = me - row0
    my_chip = pos // 2
    my_core = pos - my_chip * 2
    mid = chips // 2

    def peer_chip(t):
        turn = (t + 1) // 2
        d = mid + turn * (1 - 2 * (t - 2 * (t // 2)))
        return lax.rem(my_chip + d, chips)

    def in_row(p):
        return {"ctx": row0 + p}

    def row_peer(k):
        return in_row(lax.rem(pos + k, row_n))

    def to_row(r):
        return {"ctx": r * row_n + pos}

    def along_z(k):
        return {"ctx": lax.rem(my_row + k, n_rows) * row_n + pos}

    def along_y(k):
        return {"head": lax.rem(my_y + k, n_head)}

    ins = [
        pltpu.make_async_copy(src, dst, in_sem.at[i])
        for i, (src, dst) in enumerate(
            (
                (docs_hbm, docs_in),
                (thr_hbm, thr_in),
                (spk_hbm, spk_in),
                (v_hbm, v_in),
                (q_hbm, q_in),
                (cot_hbm, cot_in),
                (gain_hbm, gain_in),
            )
        )
    ]
    for cp in ins[:4]:
        cp.start()

    barrier = pltpu.get_barrier_semaphore()

    def greet_row(k, c):
        pl.semaphore_signal(
            barrier, inc=1, device_id=in_row(lax.rem(pos + k, row_n)), device_id_type=MESH
        )
        return c

    def greet_y(k, c):
        pl.semaphore_signal(barrier, inc=1, device_id=along_y(k), device_id_type=MESH)
        return c

    lax.fori_loop(1, row_n, greet_row, 0)
    for k in (1, 2):

        @pl.when(my_row >= k)
        def _():
            pl.semaphore_signal(barrier, inc=1, device_id=to_row(my_row - k), device_id_type=MESH)

        @pl.when(my_row + k < n_rows)
        def _():
            pl.semaphore_signal(barrier, inc=1, device_id=to_row(my_row + k), device_id_type=MESH)

    if n_head > 1:
        lax.fori_loop(1, n_head, greet_y, 0)

    for k in range(2):

        @pl.when(my_row <= k)
        def _():
            zr_f[k] = jnp.full((pr + 8, width), -1.0, F32)

        @pl.when(my_row + k >= n_rows - 1)
        def _():
            zr_b[k] = jnp.full((pr + 8, width), -1.0, F32)

    ins[0].wait()
    ins[1].wait()
    doc_row = docs_in[...].astype(F32)
    docT[...] = jnp.transpose(jnp.broadcast_to(doc_row, (width, length)))
    head_doc = docT[0:1, :]
    tail_doc = docT[length - 1 : length, :]
    ends = jnp.concatenate([head_doc, tail_doc], axis=0)
    meta_my[...] = ends
    meta[pl.ds(pos, 1)] = ends.reshape(1, 2, width)
    thr = thr_in[...]
    thr_col = jnp.transpose(jnp.broadcast_to(thr, (width, width)))

    near = jnp.minimum(my_row, 2) + jnp.minimum(n_rows - 1 - my_row, 2)
    pl.semaphore_wait(barrier, (row_n - 1) + (n_head - 1) + near)

    def send_meta(t, c):
        chip = peer_chip(t)
        for core in range(2):
            pltpu.make_async_remote_copy(
                src_ref=meta_my,
                dst_ref=meta.at[pos],
                send_sem=meta_s,
                recv_sem=meta_r,
                device_id=in_row(chip * 2 + core),
                device_id_type=MESH,
            ).start()
        return c

    lax.fori_loop(0, chips - 1, send_meta, 0)

    def to_partner(src, dst, i):
        return pltpu.make_async_remote_copy(
            src_ref=src,
            dst_ref=dst,
            send_sem=swap_s.at[i],
            recv_sem=swap_r.at[i],
            device_id=in_row(my_chip * 2 + 1 - my_core),
            device_id_type=MESH,
        )

    own_ends = to_partner(meta_my, meta.at[pos], 2)
    own_ends.start()

    def scatter(h, tail, recv, way):
        def piece(chip):
            return tail.at[pl.ds(h * width + chip * pr, pr)]

        def one(chip):
            pltpu.make_async_remote_copy(
                src_ref=piece(chip),
                dst_ref=recv.at[pos],
                send_sem=st1_s.at[way],
                recv_sem=st1_r.at[way],
                device_id=in_row(chip * 2 + h),
                device_id_type=MESH,
            ).start()

        def body(t, c):
            one(peer_chip(t))
            return c

        lax.fori_loop(0, chips - 1, body, 0)

        @pl.when(my_core != h)
        def _():
            one(my_chip)

        @pl.when(my_core == h)
        def _():
            recv[pl.ds(pos, 1)] = tail[pl.ds(h * width + my_chip * pr, pr), :].reshape(
                1, pr, width
            )

    def scatter_descriptor(recv, way):
        return pltpu.make_async_remote_copy(
            src_ref=recv.at[pl.ds(0, row_n - 1)],
            dst_ref=recv.at[pl.ds(0, row_n - 1)],
            send_sem=st1_s.at[way],
            recv_sem=st1_r.at[way],
            device_id=in_row(lax.rem(pos + 1, row_n)),
            device_id_type=MESH,
        )

    def gather(send, land, way):
        at = my_core * width + my_chip * pr

        def one(p, rsem):
            pltpu.make_async_remote_copy(
                src_ref=send.at[p],
                dst_ref=land.at[pl.ds(at, pr)],
                send_sem=st3_s.at[way],
                recv_sem=rsem,
                device_id=in_row(p),
                device_id_type=MESH,
            ).start()

        def body(t, c):
            chip = peer_chip(t)
            for core in range(2):
                one(chip * 2 + core, st3_r.at[way, my_core])
            return c

        lax.fori_loop(0, chips - 1, body, 0)
        one(my_chip * 2 + 1 - my_core, st3_p.at[way])
        land[pl.ds(at, pr), :] = send[pl.ds(pos, 1)].reshape(pr, width)

    def gather_wait_chips(land, way, h):
        part = land.at[pl.ds(0, (chips - 1) * pr)]
        pltpu.make_async_remote_copy(
            src_ref=part,
            dst_ref=part,
            send_sem=st3_s.at[way],
            recv_sem=st3_r.at[way, h],
            device_id=in_row(lax.rem(pos + 1, row_n)),
            device_id_type=MESH,
        ).wait_recv()

    def gather_wait_partner(land, way):
        part = land.at[pl.ds(0, pr)]
        pltpu.make_async_remote_copy(
            src_ref=part,
            dst_ref=part,
            send_sem=st3_s.at[way],
            recv_sem=st3_p.at[way],
            device_id=in_row(lax.rem(pos + 1, row_n)),
            device_id_type=MESH,
        ).wait_recv()

    def row_hop(k, zs, zr, way):
        step = k * (1 - 2 * way)
        copy = pltpu.make_async_remote_copy(
            src_ref=zs,
            dst_ref=zr.at[k - 1],
            send_sem=st2_s.at[way, k - 1],
            recv_sem=st2_r.at[way, k - 1],
            device_id=to_row(my_row + step),
            device_id_type=MESH,
        )
        ahead = my_row + k < n_rows
        behind = my_row >= k
        return (copy, behind, ahead) if way else (copy, ahead, behind)

    def hops_start(hops):
        for copy, sends, _ in hops:
            pl.when(sends)(copy.start)

    def hops_wait_recv(hops):
        for copy, _, receives in hops:
            pl.when(receives)(copy.wait_recv)

    def hops_wait_send(hops):
        for copy, sends, _ in hops:
            pl.when(sends)(copy.wait_send)

    def with_mark(total, mark):
        return jnp.concatenate([total, jnp.broadcast_to(mark, (8, width))], axis=0)

    for cp in ins[4:]:
        cp.start()
    ins[2].wait()
    ins[3].wait()
    v_st[...] = v_in[...].astype(F32)
    first_f = (docT[...] == head_doc).astype(F32)
    last_f = (docT[...] == tail_doc).astype(F32)
    for h in range(heads):
        lane = pl.ds(h, length, stride=heads)
        spk = spk_in[lane, :].astype(F32)
        vals = v_st[lane, :].astype(BF16)
        vb[h] = vals
        tail_f[pl.ds(h * width, width), :] = mm((spk * last_f).astype(BF16), vals, 0, 0)
        sb[h] = spk.astype(BF16)
        kb[h] = (spk * thr).astype(BF16)

    mine = pl.ds(pl.multiple_of(my_core * width, width), width)
    theirs = pl.ds(pl.multiple_of((1 - my_core) * width, width), width)
    for_theirs = to_partner(tail_f.at[theirs], ptail.at[theirs], 0)
    for_theirs.start()
    own_sums = to_partner(tail_f.at[mine], ptail.at[mine], 3)
    own_sums.start()
    own_ends.wait_recv()
    other = meta[pl.ds(my_chip * 2 + 1 - my_core, 1)].reshape(2, width)
    same_end = (other[1:2, :] == tail_doc).astype(F32)
    second = (my_core == 1).astype(F32)
    own_part = same_end + second * (1.0 - same_end)
    their_part = 1.0 + second * (same_end - 1.0)
    for_theirs.wait_recv()
    chip_f[...] = own_part * tail_f[mine, :] + their_part * ptail[mine, :]

    def chip_piece(t, c):
        chip = peer_chip(t)
        pltpu.make_async_remote_copy(
            src_ref=chip_f.at[pl.ds(chip * pr, pr)],
            dst_ref=recv_f.at[my_chip],
            send_sem=st1_s.at[0],
            recv_sem=st1_r.at[0],
            device_id=in_row(chip * 2 + my_core),
            device_id_type=MESH,
        ).start()
        return c

    lax.fori_loop(0, chips - 1, chip_piece, 0)
    recv_f[pl.ds(my_chip, 1)] = chip_f[pl.ds(my_chip * pr, pr), :].reshape(1, pr, width)
    pieces_f = pltpu.make_async_remote_copy(
        src_ref=recv_f.at[pl.ds(0, chips - 1)],
        dst_ref=recv_f.at[pl.ds(0, chips - 1)],
        send_sem=st1_s.at[0],
        recv_sem=st1_r.at[0],
        device_id=row_peer(1),
        device_id_type=MESH,
    )

    for cp in ins[4:]:
        cp.wait()
    gain = gain_in[...]
    q_st[...] = q_in[...].astype(F32)
    cot_st[...] = cot_in[...].astype(F32)
    s_at = lax.broadcasted_iota(jnp.int32, (length, length), 0)
    t_at = lax.broadcasted_iota(jnp.int32, (length, length), 1)
    doc_s = jnp.concatenate([docT[...]] * (length // width), axis=1)
    mask[...] = ((t_at <= s_at) & (doc_s == doc_row)).astype(F32)
    for h in range(heads):
        lane = pl.ds(h, length, stride=heads)
        qf = q_st[lane, :]
        qb[h] = qf.astype(BF16)
        qf1[h] = (qf * first_f).astype(BF16)
        cot = cot_st[lane, :]
        cot_h[h] = cot
        up_h[h] = cot * gain
        q_h[h] = qf
        sc = (mm(qb[h], kb[h], 1, 1) * mask[...]).astype(BF16)
        scores[h] = sc
        base[h] = qf + mm(sc, vb[h], 1, 0)

    pltpu.make_async_remote_copy(
        src_ref=meta.at[pl.ds(0, row_n - 2)],
        dst_ref=meta.at[pl.ds(0, row_n - 2)],
        send_sem=meta_s,
        recv_sem=meta_r,
        device_id=in_row(lax.rem(pos + 1, row_n)),
        device_id_type=MESH,
    ).wait_recv()
    pieces_f.wait_recv()
    row_end = meta[row_n - 1, 1:2, :]
    run = recv_f[chips - 1]
    for j in range(chips - 1):
        run = run + jnp.where(meta[2 * j + 1, 1:2, :] == row_end, recv_f[j], 0.0)
    zs_f[...] = with_mark(run, row_end)
    hops_f = [row_hop(k, zs_f, zr_f, 0) for k in (1, 2)]
    hops_start(hops_f)
    run = recv_f[0]
    before = meta[1, 1:2, :]
    send_f[0] = jnp.zeros((pr, width), F32)
    for j in range(1, chips):
        head_j, tail_j = meta[2 * j, 0:1, :], meta[2 * j + 1, 1:2, :]
        send_f[j] = jnp.where(before == head_j, run, 0.0)
        run = recv_f[j] + jnp.where(before == tail_j, run, 0.0)
        before = tail_j
    hops_wait_recv(hops_f)
    z1, z2 = zr_f[0, 0:pr, :], zr_f[1, 0:pr, :]
    m1, m2 = zr_f[0, pr : pr + 1, :], zr_f[1, pr : pr + 1, :]
    for j in range(chips):
        head_j = meta[2 * j, 0:1, :]
        send_f[j] = (
            send_f[j] + jnp.where(m1 == head_j, z1, 0.0) + jnp.where(m2 == head_j, z2, 0.0)
        )

    def enter_chip(t, c):
        chip = peer_chip(t)
        pltpu.make_async_remote_copy(
            src_ref=send_f.at[chip],
            dst_ref=land.at[my_core, pl.ds(my_chip * pr, pr)],
            send_sem=st3_s.at[0],
            recv_sem=st3_r.at[0, 0],
            device_id=in_row(chip * 2 + my_core),
            device_id_type=MESH,
        ).start()
        return c

    lax.fori_loop(0, chips - 1, enter_chip, 0)
    land[pl.ds(my_core, 1), pl.ds(my_chip * pr, pr), :] = send_f[pl.ds(my_chip, 1)]
    entered = pltpu.make_async_remote_copy(
        src_ref=send_f.at[pl.ds(0, chips - 1)],
        dst_ref=send_f.at[pl.ds(0, chips - 1)],
        send_sem=st3_s.at[0],
        recv_sem=st3_r.at[0, 0],
        device_id=row_peer(1),
        device_id_type=MESH,
    )

    @pl.when(my_row > 0)
    def _():
        pl.semaphore_wait(token, 1)

    @pl.when(my_row < n_rows - 1)
    def _():
        pl.semaphore_signal(token, inc=1, device_id=to_row(my_row + 1), device_id_type=MESH)

    def greet_below(r, c):
        pl.semaphore_signal(hello, inc=1, device_id=to_row(r), device_id_type=MESH)
        return c

    lax.fori_loop(0, my_row, greet_below, 0)

    own_sums.wait_recv()
    joins = (other[1:2, :] == head_doc).astype(F32)
    whole = (other[0:1, :] == other[1:2, :]).astype(F32)
    by_partner = joins * second
    by_entry = 1.0 + second * (joins * whole - 1.0)

    gain_term = jnp.zeros((1, width), F32)
    cross = jnp.zeros((1, width), F32)
    entered.wait_recv()
    swap = to_partner(land.at[my_core], land.at[my_core], 1)
    swap.start()
    for turn in range(2):
        h = my_core if turn == 0 else 1 - my_core
        rows = pl.ds(pl.multiple_of(h * width, width), width)
        if turn == 1:
            swap.wait_recv()
        cs = by_entry * land[h] + by_partner * ptail[rows, :]
        mixed = base[h] + mm(qf1[h], (cs * thr_col).astype(BF16), 1, 0)
        upstream = up_h[h]
        power = jnp.mean(mixed * mixed, axis=-1, keepdims=True)
        along = jnp.mean(mixed * upstream, axis=-1, keepdims=True)
        ratio = lax.rsqrt(power + 1e-06)
        normed = mixed * ratio
        g = (ratio * upstream - normed * (ratio * (ratio * along))).astype(BF16)
        gb[h] = g
        ds = (mm(g, vb[h], 1, 1) * mask[...]).astype(BF16)
        back = mm(ds, sb[h], 1, 0) + first_f * mm(g, cs.astype(BF16), 1, 1)
        back_h[h] = back
        cross = cross + jnp.sum(q_h[h] * back, axis=0, keepdims=True)
        gain_term = gain_term + jnp.sum(cot_h[h] * normed, axis=0, keepdims=True)
        att_h[h] = normed * gain

    def total_copy(buf, mine, stage, device):
        return pltpu.make_async_remote_copy(
            src_ref=buf.at[mine],
            dst_ref=buf.at[mine],
            send_sem=ar_s.at[stage],
            recv_sem=ar_r.at[stage],
            device_id=device,
            device_id_type=MESH,
        )

    def total_start(buf, count, mine, stage, device, value):
        buf[pl.ds(mine, 1)] = value.reshape(1, 2, width)

        def body(t, c):
            far_first = count // 2 + ((t + 1) // 2) * (1 - 2 * (t - 2 * (t // 2)))
            k = t + 1 if stage == 2 else far_first
            total_copy(buf, mine, stage, device(k)).start()
            return c

        lax.fori_loop(0, count - 1, body, 0)

    def total_descriptor(buf, count, stage, device):
        part = buf.at[pl.ds(0, count - 1)]
        return pltpu.make_async_remote_copy(
            src_ref=part,
            dst_ref=part,
            send_sem=ar_s.at[stage],
            recv_sem=ar_r.at[stage],
            device_id=device(1),
            device_id_type=MESH,
        )

    total_start(ar_x, row_n, pos, 0, row_peer, jnp.concatenate([cross, gain_term], axis=0))

    for h in range(heads):
        tail_b[pl.ds(h * width, width), :] = mm(qf1[h], gb[h], 0, 0)
        scatter(h, tail_b, recv_b, 1)

    for h in range(heads):
        lane = pl.ds(h, length, stride=heads)
        att_st[lane, :] = att_h[h]
        g = gb[h]
        out_st[lane, :] = g.astype(F32) + thr * back_h[h]
        vgrad[h] = mm(scores[h], g, 0, 0)
    att_ref[...] = att_st[...].astype(BF16)
    qg_ref[...] = out_st[...].astype(BF16)

    total_descriptor(ar_x, row_n, 0, row_peer).wait_recv()
    total = jnp.sum(ar_x[...], axis=0)
    if n_head > 1:
        total_start(ar_y, n_head, my_y, 1, along_y, total)

    scatter_descriptor(recv_b, 1).wait_recv()
    run = recv_b[row_n - 1]
    after = meta[row_n - 1, 0:1, :]
    send_b[row_n - 1] = jnp.zeros((pr, width), F32)
    for j in range(row_n - 2, -1, -1):
        head_j, tail_j = meta[j, 0:1, :], meta[j, 1:2, :]
        send_b[j] = jnp.where(after == tail_j, run, 0.0)
        run = recv_b[j] + jnp.where(after == head_j, run, 0.0)
        after = head_j
    zs_b[...] = with_mark(run, after)
    hops_b = [row_hop(k, zs_b, zr_b, 1) for k in (1, 2)]
    hops_start(hops_b)

    if n_head > 1:
        total_descriptor(ar_y, n_head, 1, along_y).wait_recv()
        total = jnp.sum(ar_y[...], axis=0)

    @pl.when(my_row < n_rows - 1)
    def _():
        pl.semaphore_wait(hello, n_rows - 1 - my_row)

    total_start(ar_z, n_rows, my_row, 2, along_z, total)

    hops_wait_recv(hops_b)
    z1, z2 = zr_b[0, 0:pr, :], zr_b[1, 0:pr, :]
    m1, m2 = zr_b[0, pr : pr + 1, :], zr_b[1, pr : pr + 1, :]
    for j in range(row_n):
        tail_j = meta[j, 1:2, :]
        send_b[j] = (
            send_b[j] + jnp.where(m1 == tail_j, z1, 0.0) + jnp.where(m2 == tail_j, z2, 0.0)
        )
    gather(send_b, retn, 1)

    for h in range(heads):
        gather_wait_chips(retn, 1, h)
        if h == 0:
            gather_wait_partner(retn, 1)
        lane = pl.ds(h, length, stride=heads)
        state = retn[pl.ds(h * width, width), :].astype(BF16)
        out_st[lane, :] = vgrad[h] + last_f * mm(kb[h], state, 1, 0)
    vg_ref[...] = out_st[...].astype(BF16)

    total_descriptor(ar_z, n_rows, 2, along_z).wait_recv()
    scale = 1.0 / math.sqrt(length * n_ctx * heads * n_head)
    grads_ref[...] = jnp.sum(ar_z[...], axis=0) * scale

    pltpu.make_async_remote_copy(
        src_ref=meta.at[pl.ds(0, row_n - 2)],
        dst_ref=meta.at[pl.ds(0, row_n - 2)],
        send_sem=meta_s,
        recv_sem=meta_r,
        device_id=row_peer(1),
        device_id_type=MESH,
    ).wait_send()
    pieces_f.wait_send()
    for_theirs.wait_send()
    own_ends.wait_send()
    scatter_descriptor(recv_b, 1).wait_send()
    own_sums.wait_send()
    entered.wait_send()
    swap.wait_send()
    pltpu.make_async_remote_copy(
        src_ref=send_b.at[pl.ds(0, row_n - 1)],
        dst_ref=send_b.at[pl.ds(0, row_n - 1)],
        send_sem=st3_s.at[1],
        recv_sem=st3_r.at[1, 0],
        device_id=row_peer(1),
        device_id_type=MESH,
    ).wait_send()
    hops_wait_send(hops_f + hops_b)
    total_descriptor(ar_x, row_n, 0, row_peer).wait_send()
    total_descriptor(ar_z, n_rows, 2, along_z).wait_send()
    if n_head > 1:
        total_descriptor(ar_y, n_head, 1, along_y).wait_send()


def put_out(att, qg, vg, grads, att_hbm, qg_hbm, vg_hbm, thr_hbm, gain_hbm, sem):
    pairs = [(grads.at[pl.ds(0, 1)], thr_hbm), (grads.at[pl.ds(1, 1)], gain_hbm)]
    half = att.shape[0] // 2
    for src, dst in ((att, att_hbm), (qg, qg_hbm), (vg, vg_hbm)):
        for part in range(2):
            rows = pl.ds(part * half, half)
            pairs.append((src.at[rows], dst.at[rows]))
    copies = [pltpu.make_async_copy(src, dst, sem.at[i]) for i, (src, dst) in enumerate(pairs)]
    for copy in copies:
        copy.start()
    for copy in copies:
        copy.wait()


def on_device(n_ctx, n_head, queries, spikes, values, threshold, norm_gain, document_ids, cotangent):
    length, heads, width = queries.shape
    dims = (n_ctx, n_head, ROW, length, heads, width)
    n_rows = n_ctx // ROW
    pr = width // (ROW // 2)
    flat = (length * heads, width)
    state = (heads * width, width)
    vmem = pl.BlockSpec(memory_space=pltpu.VMEM)
    hbm = pl.BlockSpec(memory_space=pl.ANY)
    dma = pltpu.SemaphoreType.DMA
    one_way = [
        pltpu.VMEM(state, F32),
        pltpu.VMEM((ROW, pr, width), F32),
        pltpu.VMEM((ROW, pr, width), F32),
        pltpu.VMEM((pr + 8, width), F32),
        pltpu.VMEM((2, pr + 8, width), F32),
        pltpu.VMEM(state, F32),
    ]
    results = pl.pallas_call(
        functools.partial(kernel, dims),
        out_shape=[pltpu.VMEM(flat, BF16)] * 3 + [pltpu.VMEM((2, width), F32)],
        in_specs=[hbm] * 7,
        out_specs=[vmem] * 4,
        scratch_shapes=[
            pltpu.VMEM((1, length), jnp.int32),
            pltpu.VMEM((1, width), F32),
            pltpu.VMEM((1, width), F32),
            pltpu.VMEM(flat, BF16),
            pltpu.VMEM(flat, jnp.int32),
            pltpu.VMEM(flat, BF16),
            pltpu.VMEM(flat, BF16),
            pltpu.VMEM(flat, F32),
            pltpu.VMEM(flat, F32),
            pltpu.VMEM(flat, F32),
            pltpu.VMEM((length, width), F32),
            pltpu.VMEM((length, length), F32),
            pltpu.VMEM((heads, length, width), BF16),
            pltpu.VMEM((heads, length, width), BF16),
            pltpu.VMEM((heads, length, width), BF16),
            pltpu.VMEM((heads, length, width), BF16),
            pltpu.VMEM((heads, length, width), BF16),
            pltpu.VMEM((heads, length, width), F32),
            pltpu.VMEM((heads, length, width), F32),
            pltpu.VMEM((heads, length, width), F32),
            pltpu.VMEM((heads, length, width), F32),
            pltpu.VMEM((heads, length, width), BF16),
            pltpu.VMEM((heads, length, width), F32),
            pltpu.VMEM(state, F32),
            pltpu.VMEM((width, width), F32),
            pltpu.VMEM((heads, width, width), F32),
            pltpu.VMEM((heads, length, length), BF16),
            pltpu.VMEM((heads, length, width), F32),
            pltpu.VMEM((heads, length, width), F32),
            pltpu.VMEM((2, width), F32),
            pltpu.VMEM((ROW, 2, width), F32),
            *one_way[:-1],
            *one_way,
            pltpu.VMEM(flat, F32),
            pltpu.VMEM(flat, F32),
            pltpu.VMEM((ROW, 2, width), F32),
            pltpu.VMEM((n_rows, 2, width), F32),
            pltpu.VMEM((max(n_head, 2), 2, width), F32),
            dma((7,)),
            dma,
            dma,
            dma((2,)),
            dma((2,)),
            dma((2, 2)),
            dma((2, 2)),
            dma((2,)),
            dma((2, 2)),
            dma((2,)),
            dma((3,)),
            dma((3,)),
            pltpu.SemaphoreType.REGULAR,
            pltpu.SemaphoreType.REGULAR,
            dma((4,)),
            dma((4,)),
        ],
        compiler_params=pltpu.CompilerParams(collective_id=0, has_side_effects=True),
    )(
        document_ids.reshape(1, length),
        threshold.reshape(1, width),
        norm_gain.reshape(1, width),
        queries.reshape(flat),
        spikes.reshape(flat),
        values.reshape(flat),
        cotangent.reshape(flat),
    )
    att, qg, vg, thr_grad, gain_grad = pl.pallas_call(
        put_out,
        out_shape=[jax.ShapeDtypeStruct(flat, BF16)] * 3 + [jax.ShapeDtypeStruct((1, width), F32)] * 2,
        in_specs=[hbm] * 4,
        out_specs=[hbm] * 5,
        scratch_shapes=[dma((8,))],
        compiler_params=pltpu.CompilerParams(vmem_limit_bytes=1 << 20),
    )(*results)
    whole = (length, heads, width)
    return (
        att.reshape(whole),
        qg.reshape(whole),
        vg.reshape(whole),
        thr_grad.reshape(width),
        gain_grad.reshape(width),
    )


def solution(mesh):
    tokens = P("ctx", "head", None)
    return jax.shard_map(
        functools.partial(on_device, mesh.shape["ctx"], mesh.shape["head"]),
        mesh=mesh,
        in_specs=(tokens, tokens, tokens, P(), P(), P("ctx"), tokens),
        out_specs=(tokens, tokens, tokens, P(), P()),
        check_vma=False,
    )
```
